128 devices in a mesh: section: 2 (over z_hi), expert: 8 (over y, z_lo), dp: 8 (over x, core).
Axes of the slice: x: 4, y: 4, z: 4 (z_hi: 2, z_lo: 2; z = z_hi * 2 + z_lo), core: 2. Of those that a mesh axis runs over, the one named last changes fastest.
Arguments:
- inputs: bfloat16 [2, 512, 3072], P(None, ('expert', 'dp')), may hold values from -6 to 6
- cotangent: bfloat16 [2, 512, 3072], P(None, ('expert', 'dp')), may hold values from -6 to 6
- norm_gain: bfloat16 [2, 3072], P('section'), may hold values from 0.5 to 1.5
- router: bfloat16 [2, 3072, 8], P('section'), may hold values from -0.109375 to 0.109375
- w_gate: bfloat16 [2, 8, 3072, 8192], P('section', 'expert', None, 'dp'), may hold values from -0.109375 to 0.109375
- w_up: bfloat16 [2, 8, 3072, 8192], P('section', 'expert', None, 'dp'), may hold values from -0.109375 to 0.109375
- w_down: bfloat16 [2, 8, 8192, 3072], P('section', 'expert', 'dp'), may hold values from -0.0625 to 0.0625
- routes: int32 [2, 2, 512, 2], P('section', None, ('expert', 'dp')), may hold values from 0 to 7, as said below
Outputs:
- acts: bfloat16 [2, 2, 512, 3072], P('section', None, ('expert', 'dp'))
- grads: bfloat16 [2, 2, 512, 3072], P('section', None, ('expert', 'dp'))
- router_grad: float32 [2, 3072, 8], P('section')
The draws below stay inside these ranges and needn't reach their ends.
Inputs may be any that keep to these rules, and one draw needn't show every extreme that they name: `routes`: the two experts of a token differ. For each layer and micro-batch, the 8 tokens of one device name no expert more than 3 times, and one expert, the same on all devices for that layer and micro-batch, exactly 3 times.
All inputs are finite; a program needn't handle non-finite values.
Results may differ from the reference program's by a relative error of at most 0.017.
Values may be sent and summed in bfloat16 or wider, within the bound.
A program may use at most 128 MiB of HBM per device.

```python
import jax
import jax.numpy as jnp
from jax import lax

D = 3072
FF = 8192
TOP = 2
MICRO = 2
TOK_DEV = 8
E = 8
LAYERS = 2
CAP = 3
TOKENS = 512
N_DP = 8


def routes_block(block_key, hot_expert):
    key_order, key_flip, key_shuffle = jax.random.split(block_key, 3)
    others = jnp.arange((E - 1) * CAP, dtype=jnp.int32) // CAP
    others = others + (others >= hot_expert).astype(jnp.int32)
    ordering = jax.random.permutation(key_order, (E - 1) * CAP)
    chosen_rest = others[ordering[:TOP * TOK_DEV - CAP]]
    merged = jnp.sort(jnp.concatenate([jnp.full((CAP,), hot_expert, jnp.int32), chosen_rest]))
    pair_table = jnp.stack([merged[:TOK_DEV], merged[TOK_DEV:]], axis=1)
    flipped = jax.random.randint(key_flip, (TOK_DEV,), 0, 2)
    pair_table = jnp.where(flipped[:, None] == 1, pair_table[:, ::-1], pair_table)
    shuffle = jax.random.permutation(key_shuffle, TOK_DEV)
    return pair_table[shuffle]


def draw_routes(key, part):
    slices = LAYERS * MICRO
    blocks = TOKENS // TOK_DEV
    hot_expert = jax.random.randint(jax.random.fold_in(key, 7), (slices,), 0, E)
    block_keys = jax.random.split(jax.random.fold_in(key, 11), slices * blocks)
    hot_each = jnp.repeat(hot_expert, blocks)
    result = jax.vmap(routes_block)(block_keys, hot_each)
    return result.reshape(LAYERS, MICRO, TOKENS, TOP).astype(jnp.int32)


def shard_levels(stream_key, dims, cuts, smallest, top_value):
    loudness, own = 1.0, jax.random.fold_in(stream_key, 6)
    for position, parts in cuts:
        draws = jnp.exp(jax.random.uniform(jax.random.fold_in(own, position), (parts,), jnp.float32, smallest / len(cuts), top_value / len(cuts)))
        loudness = loudness * jnp.repeat(draws, dims[position] // parts).reshape([-1 if axis == position else 1 for axis in range(len(dims))])
    return loudness


def gaussian(key, extent, width, most, pieces=(), kind=jnp.bfloat16):
    values = jax.random.normal(key, extent, jnp.float32) * width
    if len(pieces) > 0:
        values = shard_levels(key, extent, pieces, -0.22, 0.18) * values
    return jnp.clip(values, min=-most, max=most).astype(kind)


def setup_inputs(seed: int = 0) -> dict:
    key_of = jax.random.split(jax.random.key(seed), 9)
    inputs = gaussian(key_of[0], (MICRO, TOKENS, D), 1.0, 6.0, ((1, 64),))
    cotangent = gaussian(key_of[1], (MICRO, TOKENS, D), 1.0, 6.0, ((1, 64),))
    norm_gain = jnp.clip(1.0 + 0.1 * jax.random.normal(key_of[2], (LAYERS, D), jnp.float32), 0.5, 1.5).astype(jnp.bfloat16)
    router = gaussian(key_of[3], (LAYERS, D, E), D ** -0.5, 0.109375, ((0, 2),))
    w_gate = gaussian(key_of[4], (LAYERS, E, D, FF), D ** -0.5, 0.109375, ((0, 2), (1, 8), (3, 8)))
    w_up = gaussian(key_of[5], (LAYERS, E, D, FF), D ** -0.5, 0.109375, ((0, 2), (1, 8), (3, 8)))
    w_down = gaussian(key_of[6], (LAYERS, E, FF, D), FF ** -0.5, 0.0625, ((0, 2), (1, 8), (2, 8)))
    routes = draw_routes(jax.random.fold_in(key_of[8], 71), 0)
    return dict(inputs=inputs, cotangent=cotangent, norm_gain=norm_gain, router=router, w_gate=w_gate, w_up=w_up, w_down=w_down, routes=routes)


EPSILON = 1e-05

def norm_rows(layer_in, gain_row):
    values = layer_in.astype(jnp.float32)
    inv_rms = lax.rsqrt(lax.optimization_barrier(jnp.mean(values * values, axis=-1, keepdims=True)) + EPSILON)
    return (values, inv_rms, (values * inv_rms * gain_row).astype(jnp.bfloat16))

def gate_probs(hidden, router_w, picks):
    logits = jnp.dot(hidden, router_w, preferred_element_type=jnp.float32)
    chosen = jnp.take_along_axis(logits, picks, axis=1)
    logit_gap = chosen[:, 0] - chosen[:, 1]
    return jnp.stack([jax.nn.sigmoid(logit_gap), jax.nn.sigmoid(-logit_gap)], axis=1)

def slot_table(picks, experts, capacity):
    flat_pick = picks.reshape(-1).astype(jnp.int32)
    onehot = (flat_pick[:, None] == jnp.arange(experts, dtype=jnp.int32)[None, :]).astype(jnp.int32)
    earlier = jnp.cumsum(onehot, axis=0) - onehot
    slot_pos = lax.optimization_barrier(jnp.sum(earlier * onehot, axis=1))
    target = flat_pick * capacity + slot_pos
    return target[:, None] == jnp.arange(experts * capacity, dtype=jnp.int32)[None, :]

def route_tables(picks):
    blocks = picks.reshape(-1, TOK_DEV, TOP)
    return jax.vmap(lambda block_picks: slot_table(block_picks, E, CAP))(blocks)

def dispatch_rows(placing, row_values):
    grouped = jnp.einsum('bsr,bsd->brd', placing.astype(jnp.float32), row_values.astype(jnp.float32), precision=lax.Precision.HIGHEST)
    grouped = grouped.astype(jnp.bfloat16).reshape(-1, E, CAP, D)
    return grouped.transpose(1, 0, 2, 3).reshape(E, -1, D)

def return_rows(placing, per_expert):
    returned = per_expert.reshape(E, -1, CAP, D).transpose(1, 0, 2, 3).reshape(-1, E * CAP, D)
    picked = jnp.einsum('bsr,brd->bsd', placing.astype(jnp.float32), returned, precision=lax.Precision.HIGHEST)
    return picked.reshape(TOKENS, TOP, D)

def expert_out(operands):
    row_block, gate_w, up_w, down_w = operands
    shard_width = gate_w.shape[1] // N_DP
    summed = jnp.zeros((row_block.shape[0], down_w.shape[1]), jnp.float32)
    for shard_no in range(N_DP):
        offset = shard_no * shard_width
        gate_pre = jnp.dot(row_block, gate_w[:, offset:offset + shard_width], preferred_element_type=jnp.float32)
        up_pre = jnp.dot(row_block, up_w[:, offset:offset + shard_width], preferred_element_type=jnp.float32)
        active = (gate_pre * jax.nn.sigmoid(gate_pre) * up_pre).astype(jnp.bfloat16)
        partial_out = jnp.dot(active, down_w[offset:offset + shard_width], preferred_element_type=jnp.float32)
        partial_out = partial_out.astype(jnp.bfloat16)
        summed = summed + lax.optimization_barrier(partial_out).astype(jnp.float32)
    return summed

def expert_grad(operands):
    row_block, grad_block, gate_w, up_w, down_w = operands
    shard_width = gate_w.shape[1] // N_DP
    summed = jnp.zeros((row_block.shape[0], gate_w.shape[0]), jnp.float32)
    for shard_no in range(N_DP):
        offset = shard_no * shard_width
        gate_slab = gate_w[:, offset:offset + shard_width]
        up_slab = up_w[:, offset:offset + shard_width]
        gate_pre = jnp.dot(row_block, gate_slab, preferred_element_type=jnp.float32)
        up_pre = jnp.dot(row_block, up_slab, preferred_element_type=jnp.float32)
        d_active = jnp.dot(grad_block, down_w[offset:offset + shard_width].T, preferred_element_type=jnp.float32)
        gate_sig = jax.nn.sigmoid(gate_pre)
        d_gate = (d_active * up_pre * gate_sig * (1.0 + gate_pre * (1.0 - gate_sig))).astype(jnp.bfloat16)
        d_up = (d_active * gate_pre * gate_sig).astype(jnp.bfloat16)
        d_rows = jnp.dot(d_gate, gate_slab.T, preferred_element_type=jnp.float32)
        d_rows = d_rows + jnp.dot(d_up, up_slab.T, preferred_element_type=jnp.float32)
        summed = summed + lax.optimization_barrier(d_rows.astype(jnp.bfloat16)).astype(jnp.float32)
    return summed

def layer_forward(layer_in, picks, gain_row, router_w, gate_w, up_w, down_w):
    values, inv_rms, hidden = norm_rows(layer_in, gain_row)
    gate_prob = gate_probs(hidden, router_w, picks)
    placing = route_tables(picks)
    repeated = jnp.repeat(hidden, TOP, axis=0).reshape(-1, TOK_DEV * TOP, D)
    per_expert = lax.map(expert_out, (dispatch_rows(placing, repeated), gate_w, up_w, down_w))
    picked = return_rows(placing, per_expert)
    layer_out = (values + lax.optimization_barrier(jnp.sum(gate_prob[:, :, None] * picked, axis=1))).astype(jnp.bfloat16)
    return (layer_out, picked)

def layer_backward(layer_in, upstream, picks, gain_row, router_w, gate_w, up_w, down_w, picked):
    values, inv_rms, hidden = norm_rows(layer_in, gain_row)
    gate_prob = gate_probs(hidden, router_w, picks)
    placing = route_tables(picks)
    grad_out = upstream.astype(jnp.float32)
    d_prob = lax.optimization_barrier(jnp.sum(grad_out[:, None, :] * picked, axis=2))
    d_gap = gate_prob[:, 0] * gate_prob[:, 1] * (d_prob[:, 0] - d_prob[:, 1])
    d_chosen = jnp.stack([d_gap, -d_gap], axis=1)
    expert_hot = (picks[:, :, None] == jnp.arange(E, dtype=jnp.int32)[None, None, :]).astype(jnp.float32)
    d_logits = lax.optimization_barrier(jnp.sum(d_chosen[:, :, None] * expert_hot, axis=1))
    scaled = (gate_prob[:, :, None] * grad_out[:, None, :]).astype(jnp.bfloat16).reshape(-1, TOK_DEV * TOP, D)
    repeated = jnp.repeat(hidden, TOP, axis=0).reshape(-1, TOK_DEV * TOP, D)
    grads_expert = lax.map(expert_grad, (dispatch_rows(placing, repeated), dispatch_rows(placing, scaled), gate_w, up_w, down_w))
    returned = return_rows(placing, grads_expert)
    d_hidden = lax.optimization_barrier(jnp.sum(returned, axis=1)) + jnp.dot(d_logits, router_w.astype(jnp.float32).T, precision=lax.Precision.HIGHEST)
    router_term = jnp.dot(hidden.astype(jnp.float32).T, d_logits, precision=lax.Precision.HIGHEST)
    weighted = gain_row * d_hidden
    cubed = inv_rms * inv_rms * inv_rms
    d_in = grad_out + inv_rms * weighted - values * cubed * lax.optimization_barrier(jnp.mean(values * weighted, axis=-1, keepdims=True))
    return (d_in.astype(jnp.bfloat16), router_term)

def reference(inputs, cotangent, norm_gain, router, w_gate, w_up, w_down, routes):
    layer_inputs = [[None] * MICRO for _ in range(LAYERS)]
    layer_outputs = [[None] * MICRO for _ in range(LAYERS)]
    stashed = [[None] * MICRO for _ in range(LAYERS)]
    for micro_no in range(MICRO):
        current = inputs[micro_no]
        for layer_no in range(LAYERS):
            layer_inputs[layer_no][micro_no] = current
            current, picked = layer_forward(current, routes[layer_no, micro_no], norm_gain[layer_no].astype(jnp.float32), router[layer_no], w_gate[layer_no], w_up[layer_no], w_down[layer_no])
            layer_outputs[layer_no][micro_no] = current
            stashed[layer_no][micro_no] = picked
    layer_grads = [[None] * MICRO for _ in range(LAYERS)]
    router_sums = [jnp.zeros((D, E), jnp.float32) for _ in range(LAYERS)]
    for micro_no in range(MICRO):
        upstream = cotangent[micro_no]
        for layer_no in reversed(range(LAYERS)):
            upstream, router_term = layer_backward(layer_inputs[layer_no][micro_no], upstream, routes[layer_no, micro_no], norm_gain[layer_no].astype(jnp.float32), router[layer_no], w_gate[layer_no], w_up[layer_no], w_down[layer_no], stashed[layer_no][micro_no])
            layer_grads[layer_no][micro_no] = upstream
            router_sums[layer_no] = router_sums[layer_no] + router_term
    acts = jnp.stack([jnp.stack(per_layer) for per_layer in layer_outputs])
    grads = jnp.stack([jnp.stack(per_layer) for per_layer in layer_grads])
    router_grad = jnp.stack(router_sums)
    return (acts, grads, router_grad)
```

```python
import jax
import jax.numpy as jnp
from jax import lax
from jax.experimental import pallas as pl
from jax.experimental.pallas import tpu as pltpu
from jax.sharding import PartitionSpec as P

EPSILON = 1e-05
MESH = pl.DeviceIdType.MESH
NT = (((1,), (1,)), ((), ()))


def sigmoid(x):
    return jax.nn.sigmoid(x)


def relay_kernel(
    dims,
    table,
    x_in,
    cot_in,
    gain_in,
    router_in,
    wg_hbm,
    wu_hbm,
    wd_hbm,
    acts,
    grads,
    rgrad,
    wg,
    wu,
    wd,
    lin,
    ups,
    hid,
    scl,
    prob,
    pdiff,
    snd,
    disp,
    xf,
    xb,
    gs,
    us,
    act,
    act2,
    obuf,
    osend,
    orecv,
    snd2,
    comb,
    racc,
    r1,
    r2,
    r3,
    rsrc,
    w_sem,
    disp_send,
    disp_recv,
    x_send,
    x_recv,
    o_send,
    o_recv,
    comb_send,
    comb_recv,
    hop_send,
    hop_recv,
    r_send,
    r_recv,
):
    n_exp, n_x, cap, toks, chunks, n_ff, n_out, width = dims
    group = n_exp * n_x
    rows = group * cap
    per_x = cap * chunks
    inv_count = 1.0 / (chunks * 128)
    n_group, k_group = xb.shape[1], xb.shape[4]
    group_chunks = k_group // 128
    none = 2 * toks

    section = lax.axis_index("section")
    my_e = lax.axis_index("expert")
    my_dp = lax.axis_index("dp")
    my_x = my_dp // 2
    core = lax.rem(my_dp, 2)
    me = my_e * n_x + my_x

    def peer(step):
        q = lax.rem(me + step, group)
        return q, {"expert": q // n_x, "dp": lax.rem(q, n_x) * 2 + core}

    sibling = {"dp": my_x * 2 + 1 - core}
    partner = {"section": 1 - section}

    weights = [
        pltpu.make_async_copy(src, dst, w_sem.at[i])
        for i, (src, dst) in enumerate(((wg_hbm, wg), (wu_hbm, wu), (wd_hbm, wd)))
    ]
    for copy in weights:
        copy.start()

    barrier = pltpu.get_barrier_semaphore()

    @pl.loop(1, group)
    def _(step):
        _, where = peer(step)
        pl.semaphore_signal(barrier, inc=1, device_id=where, device_id_type=MESH)

    @pl.loop(0, n_x)
    def _(x):
        pl.semaphore_signal(
            barrier, inc=1, device_id={"dp": x * 2 + 1 - core}, device_id_type=MESH
        )

    pl.semaphore_signal(barrier, inc=1, device_id=partner, device_id_type=MESH)

    @pl.when(section == 0)
    def _():
        lin[...] = x_in[...]

    @pl.when(section == 1)
    def _():
        ups[...] = cot_in[...]

    hid[:, toks] = jnp.zeros_like(hid[:, toks])
    scl[:, none] = jnp.zeros_like(scl[:, none])
    pl.semaphore_wait(barrier, group + n_x)

    gain = gain_in[...]

    def total(v):
        return jnp.sum(v, axis=(0, 1), keepdims=True)

    def inv_rms_of(v):
        return lax.rsqrt(total(v * v) * inv_count + EPSILON)

    def wait_bytes(ref, sem):
        pltpu.make_async_copy(ref, ref, sem).wait()

    def route(m, t, k):
        return table[m, n_exp * cap + none + 2 * t + k]

    def router_diff(m, t):
        return router_in[route(m, t, 0)] - router_in[route(m, t, 1)]

    def send_dispatch(phase):
        own = pltpu.make_async_copy(snd.at[phase, my_e], disp.at[phase, me], disp_recv.at[phase])
        own.start()

        @pl.loop(1, group)
        def _(step):
            q, where = peer(step)
            pltpu.make_async_remote_copy(
                src_ref=snd.at[phase, q // n_x],
                dst_ref=disp.at[phase, me],
                send_sem=disp_send.at[phase],
                recv_sem=disp_recv.at[phase],
                device_id=where,
                device_id_type=MESH,
            ).start()

    def send_combine(phase):
        own = pltpu.make_async_copy(snd2.at[phase, me], comb.at[phase, me], comb_recv.at[phase])
        own.start()

        @pl.loop(1, group)
        def _(step):
            q, where = peer(step)
            pltpu.make_async_remote_copy(
                src_ref=snd2.at[phase, q],
                dst_ref=comb.at[phase, me],
                send_sem=comb_send.at[phase],
                recv_sem=comb_recv.at[phase],
                device_id=where,
                device_id_type=MESH,
            ).start()

    def hop(ref, dst, which, m):
        return pltpu.make_async_remote_copy(
            src_ref=ref.at[m],
            dst_ref=dst.at[m],
            send_sem=hop_send.at[which, m],
            recv_sem=hop_recv.at[which, m],
            device_id=partner,
            device_id_type=MESH,
        )

    def take_rows(phase):
        wait_bytes(disp.at[phase], disp_recv.at[phase])

        @pl.loop(0, group)
        def _(q):
            block = disp[phase, q].astype(jnp.float32).reshape(per_x, 128)
            xf[pl.ds(pl.multiple_of(q * per_x, 8), per_x), :] = block

        for g in range(n_group):
            for i in range(group_chunks):
                part = xf[pl.ds(g * group_chunks + i, rows, stride=chunks), :]
                xb[phase, g, core, :, i * 128 : (i + 1) * 128] = part.astype(jnp.bfloat16)
            pltpu.make_async_remote_copy(
                src_ref=xb.at[phase, g, core],
                dst_ref=xb.at[phase, g, core],
                send_sem=x_send.at[phase, g],
                recv_sem=x_recv.at[phase, g],
                device_id=sibling,
                device_id_type=MESH,
            ).start()
        for g in range(n_group):
            wait_bytes(xb.at[phase, g, 1 - core], x_recv.at[phase, g])

    def left(phase, g):
        return xb[phase, g].reshape(2 * rows, k_group)

    def share_tile(phase, n, tile):
        obuf[n] = tile.reshape(2, rows, 256)
        osend[phase, n] = obuf[n, 1 - core].astype(jnp.bfloat16)
        pltpu.make_async_remote_copy(
            src_ref=osend.at[phase, n],
            dst_ref=orecv.at[phase, n],
            send_sem=o_send.at[phase],
            recv_sem=o_recv.at[phase],
            device_id=sibling,
            device_id_type=MESH,
        ).start()

    def give_back(phase):
        wait_bytes(orecv.at[phase], o_recv.at[phase])
        for n in range(n_out):
            both = obuf[n, core] + orecv[phase, n].astype(jnp.float32)
            for i in range(2):
                xf[pl.ds(2 * n + i, rows, stride=chunks), :] = both[:, i * 128 : (i + 1) * 128]

        @pl.loop(0, group)
        def _(q):
            block = xf[pl.ds(pl.multiple_of(q * per_x, 8), per_x), :]
            snd2[phase, q] = block.reshape(cap, chunks, 128).astype(jnp.bfloat16)

        send_combine(phase)

    def fill_slots(phase, m, source, shift):
        for e in range(n_exp):
            for s in range(cap):
                snd[phase, e, s] = source[m, table[m, e * cap + s] >> shift]

    def picked_of(phase, m, t, k):
        slot = table[m, n_exp * cap + 2 * t + k]
        e, s = slot // cap, lax.rem(slot, cap)
        result = comb[phase, e * n_x, s].astype(jnp.float32)
        for x in range(1, n_x):
            result = result + comb[phase, e * n_x + x, s].astype(jnp.float32)
        return result

    def forward_send(m):
        @pl.when(section == 1)
        def _():
            hop(acts, lin, 0, m).wait_recv()

        for t in range(toks):
            v = lin[m, t].astype(jnp.float32)
            hidden = (v * inv_rms_of(v) * gain).astype(jnp.bfloat16)
            hid[m, t] = hidden
            gap = total(hidden.astype(jnp.float32) * router_diff(m, t))
            prob[m, t, 0] = jnp.broadcast_to(sigmoid(gap), (8, 128))
            prob[m, t, 1] = jnp.broadcast_to(sigmoid(-gap), (8, 128))
        fill_slots(m, m, hid, 1)
        send_dispatch(m)

    def forward_expert(m):
        take_rows(m)
        if m == 0:
            weights[0].wait()
            weights[1].wait()

        @pl.loop(0, n_ff)
        def _(n):
            cols = pl.ds(pl.multiple_of(n * 256, 256), 256)
            gate = jnp.zeros((2 * rows, 256), jnp.float32)
            up = jnp.zeros((2 * rows, 256), jnp.float32)
            for g in range(n_group):
                x = left(m, g)
                k = slice(g * k_group, (g + 1) * k_group)
                gate = gate + jnp.dot(x, wg[k, cols], preferred_element_type=jnp.float32)
                up = up + jnp.dot(x, wu[k, cols], preferred_element_type=jnp.float32)
            gs[m, n] = gate
            us[m, n] = up
            act[n] = (gate * sigmoid(gate) * up).astype(jnp.bfloat16)

        if m == 0:
            weights[2].wait()

        @pl.loop(0, n_out)
        def _(n):
            cols = pl.ds(pl.multiple_of(n * 256, 256), 256)
            tile = jnp.zeros((2 * rows, 256), jnp.float32)
            for k in range(n_ff):
                tile = tile + jnp.dot(
                    act[k], wd[k * 256 : (k + 1) * 256, cols], preferred_element_type=jnp.float32
                )
            share_tile(m, n, tile)

        give_back(m)

    def forward_end(m):
        wait_bytes(comb.at[m], comb_recv.at[m])
        for t in range(toks):
            p0 = prob[m, t, 0, 0:1, 0:1]
            p1 = prob[m, t, 1, 0:1, 0:1]
            one, two = picked_of(m, m, t, 0), picked_of(m, m, t, 1)
            v = lin[m, t].astype(jnp.float32)
            acts[m, t] = (v + (p0 * one + p1 * two)).astype(jnp.bfloat16)
            pdiff[m, t] = one - two

        @pl.when(section == 0)
        def _():
            hop(acts, lin, 0, m).start()

    def backward_send(m):
        phase = 2 + m

        @pl.when(section == 0)
        def _():
            hop(grads, ups, 1, m).wait_recv()

        gaps = []
        for t in range(toks):
            up = ups[m, t].astype(jnp.float32)
            p0 = prob[m, t, 0, 0:1, 0:1]
            p1 = prob[m, t, 1, 0:1, 0:1]
            d_gap = p0 * p1 * total(up * pdiff[m, t])
            prob[m, t, 2] = jnp.broadcast_to(d_gap, (8, 128))
            gaps.append(d_gap)
            scl[m, 2 * t] = (p0 * up).astype(jnp.bfloat16)
            scl[m, 2 * t + 1] = (p1 * up).astype(jnp.bfloat16)
        fill_slots(phase, m, scl, 0)
        send_dispatch(phase)
        for e in range(n_exp):
            term = racc[e] if m else jnp.zeros((chunks, 128), jnp.float32)
            for t in range(toks):
                sign = jnp.where(route(m, t, 0) == e, 1.0, 0.0) - jnp.where(
                    route(m, t, 1) == e, 1.0, 0.0
                )
                term = term + (gaps[t] * sign) * hid[m, t].astype(jnp.float32)
            racc[e] = term

    def router_one():
        pltpu.make_async_copy(racc.at[my_e], r1.at[my_e], r_recv.at[0]).start()

        @pl.loop(1, n_exp)
        def _(step):
            e = lax.rem(my_e + step, n_exp)
            pltpu.make_async_remote_copy(
                src_ref=racc.at[e],
                dst_ref=r1.at[my_e],
                send_sem=r_send.at[0],
                recv_sem=r_recv.at[0],
                device_id={"expert": e},
                device_id_type=MESH,
            ).start()

    def router_two():
        wait_bytes(r1, r_recv.at[0])
        rsrc[0] = jnp.sum(r1[...], axis=0)
        pltpu.make_async_copy(rsrc.at[0], r2.at[my_dp], r_recv.at[1]).start()

        @pl.loop(1, 2 * n_x)
        def _(step):
            dp = lax.rem(my_dp + step, 2 * n_x)
            pltpu.make_async_remote_copy(
                src_ref=rsrc.at[0],
                dst_ref=r2.at[my_dp],
                send_sem=r_send.at[1],
                recv_sem=r_recv.at[1],
                device_id={"dp": dp},
                device_id_type=MESH,
            ).start()

    def router_three():
        wait_bytes(r2, r_recv.at[1])
        rsrc[1] = jnp.sum(r2[...], axis=0)
        pltpu.make_async_copy(rsrc.at[1], r3.at[my_e], r_recv.at[2]).start()

        @pl.loop(1, n_exp)
        def _(step):
            e = lax.rem(my_e + step, n_exp)
            pltpu.make_async_remote_copy(
                src_ref=rsrc.at[1],
                dst_ref=r3.at[my_e],
                send_sem=r_send.at[2],
                recv_sem=r_recv.at[2],
                device_id={"expert": e},
                device_id_type=MESH,
            ).start()

    def backward_expert(m):
        phase = 2 + m
        take_rows(phase)

        @pl.loop(0, n_ff)
        def _(n):
            part = pl.ds(pl.multiple_of(n * 256, 256), 256)
            d_act = jnp.zeros((2 * rows, 256), jnp.float32)
            for g in range(n_group):
                d_act = d_act + lax.dot_general(
                    left(phase, g),
                    wd[part, g * k_group : (g + 1) * k_group],
                    NT,
                    preferred_element_type=jnp.float32,
                )
            gate, up = gs[m, n], us[m, n]
            sig = sigmoid(gate)
            act[n] = (d_act * up * sig * (1.0 + gate * (1.0 - sig))).astype(jnp.bfloat16)
            act2[n] = (d_act * gate * sig).astype(jnp.bfloat16)

        if m:
            router_two()

        @pl.loop(0, n_out)
        def _(n):
            part = pl.ds(pl.multiple_of(n * 256, 256), 256)
            tile = jnp.zeros((2 * rows, 256), jnp.float32)
            for k in range(n_ff):
                cols = slice(k * 256, (k + 1) * 256)
                tile = tile + lax.dot_general(
                    act[k], wg[part, cols], NT, preferred_element_type=jnp.float32
                )
                tile = tile + lax.dot_general(
                    act2[k], wu[part, cols], NT, preferred_element_type=jnp.float32
                )
            share_tile(phase, n, tile)

        give_back(phase)
        if m:
            router_three()

    def backward_end(m):
        phase = 2 + m
        wait_bytes(comb.at[phase], comb_recv.at[phase])
        for t in range(toks):
            d_gap = prob[m, t, 2, 0:1, 0:1]
            d_hidden = picked_of(phase, m, t, 0) + picked_of(phase, m, t, 1)
            d_hidden = d_hidden + d_gap * router_diff(m, t)
            v = lin[m, t].astype(jnp.float32)
            up = ups[m, t].astype(jnp.float32)
            inv_rms = inv_rms_of(v)
            weighted = gain * d_hidden
            mean = total(v * weighted) * inv_count
            d_in = up + inv_rms * weighted - v * (inv_rms * inv_rms * inv_rms) * mean
            grads[m, t] = d_in.astype(jnp.bfloat16)

        @pl.when(section == 1)
        def _():
            hop(grads, ups, 1, m).start()

    for m in range(2):
        forward_send(m)
        forward_expert(m)
        forward_end(m)
    for m in range(2):
        backward_send(m)
        if m:
            router_one()
        backward_expert(m)
        backward_end(m)
    wait_bytes(r3, r_recv.at[2])
    rgrad[...] = r3[...]

    for phase in range(4):
        wait_bytes(disp.at[phase, pl.ds(0, group - 1)], disp_send.at[phase])
        wait_bytes(comb.at[phase, pl.ds(0, group - 1)], comb_send.at[phase])
        for g in range(n_group):
            wait_bytes(xb.at[phase, g, core], x_send.at[phase, g])
        wait_bytes(osend.at[phase], o_send.at[phase])
    wait_bytes(r1.at[pl.ds(0, n_exp - 1)], r_send.at[0])
    wait_bytes(r2.at[pl.ds(0, 2 * n_x - 1)], r_send.at[1])
    wait_bytes(r1.at[pl.ds(0, n_exp - 1)], r_send.at[2])
    for m in range(2):

        @pl.when(section == 0)
        def _():
            hop(acts, lin, 0, m).wait_send()

        @pl.when(section == 1)
        def _():
            hop(grads, ups, 1, m).wait_send()


def slot_tables(picks, cap, experts):
    micro, toks, top = picks.shape
    flat = picks.reshape(micro, toks * top)
    order = jnp.arange(toks * top, dtype=jnp.int32)
    same = (flat[:, :, None] == flat[:, None, :]) & (order[None, None, :] < order[None, :, None])
    slot_of = flat * cap + jnp.sum(same.astype(jnp.int32), axis=2)
    slots = jnp.arange(experts * cap, dtype=jnp.int32)
    hit = slot_of[:, None, :] == slots[None, :, None]
    gap = toks * top - order
    slot_src = toks * top - jnp.sum(jnp.where(hit, gap[None, None, :], 0), axis=2)
    return jnp.concatenate([slot_src, slot_of, flat], axis=1).astype(jnp.int32)


def per_device(inputs, cotangent, norm_gain, router, w_gate, w_up, w_down, routes):
    micro, toks, width = inputs.shape
    experts = router.shape[2]
    dp = lax.axis_size("dp")
    n_exp, n_x = lax.axis_size("expert"), dp // 2
    cap = 3
    chunks = width // 128
    hidden_units = w_gate.shape[3]
    n_ff, n_out = hidden_units // 256, width // 256
    group = n_exp * n_x
    rows = group * cap
    n_group = 4
    k_group = width // n_group
    table = slot_tables(routes[0], cap, experts)
    bf, f32 = jnp.bfloat16, jnp.float32
    block = (chunks, 128)
    dma = pltpu.SemaphoreType.DMA
    scratch = [
        pltpu.VMEM((width, hidden_units), bf),
        pltpu.VMEM((width, hidden_units), bf),
        pltpu.VMEM((hidden_units, width), bf),
        pltpu.VMEM((micro, toks) + block, bf),
        pltpu.VMEM((micro, toks) + block, bf),
        pltpu.VMEM((micro, toks + 1) + block, bf),
        pltpu.VMEM((micro, 2 * toks + 1) + block, bf),
        pltpu.VMEM((micro, toks, 3, 8, 128), f32),
        pltpu.VMEM((micro, toks) + block, f32),
        pltpu.VMEM((4, n_exp, cap) + block, bf),
        pltpu.VMEM((4, group, cap) + block, bf),
        pltpu.VMEM((rows * chunks, 128), f32),
        pltpu.VMEM((4, n_group, 2, rows, k_group), bf),
        pltpu.VMEM((micro, n_ff, 2 * rows, 256), f32),
        pltpu.VMEM((micro, n_ff, 2 * rows, 256), f32),
        pltpu.VMEM((n_ff, 2 * rows, 256), bf),
        pltpu.VMEM((n_ff, 2 * rows, 256), bf),
        pltpu.VMEM((n_out, 2, rows, 256), f32),
        pltpu.VMEM((4, n_out, rows, 256), bf),
        pltpu.VMEM((4, n_out, rows, 256), bf),
        pltpu.VMEM((4, group, cap) + block, bf),
        pltpu.VMEM((4, group, cap) + block, bf),
        pltpu.VMEM((n_exp,) + block, f32),
        pltpu.VMEM((n_exp,) + block, f32),
        pltpu.VMEM((dp,) + block, f32),
        pltpu.VMEM((n_exp,) + block, f32),
        pltpu.VMEM((2,) + block, f32),
        dma((3,)),
        dma((4,)),
        dma((4,)),
        dma((4, n_group)),
        dma((4, n_group)),
        dma((4,)),
        dma((4,)),
        dma((4,)),
        dma((4,)),
        dma((2, micro)),
        dma((2, micro)),
        dma((3,)),
        dma((3,)),
    ]
    dims = (n_exp, n_x, cap, toks, chunks, n_ff, n_out, width)
    vmem = pl.BlockSpec(memory_space=pltpu.VMEM)
    hbm = pl.BlockSpec(memory_space=pl.ANY)
    acts, grads, rgrad = pl.pallas_call(
        lambda *refs: relay_kernel(dims, *refs),
        out_shape=(
            jax.ShapeDtypeStruct((micro, toks) + block, bf),
            jax.ShapeDtypeStruct((micro, toks) + block, bf),
            jax.ShapeDtypeStruct((experts,) + block, f32),
        ),
        in_specs=[pl.BlockSpec(memory_space=pltpu.SMEM)] + [vmem] * 4 + [hbm] * 3,
        out_specs=(vmem, vmem, vmem),
        scratch_shapes=scratch,
        compiler_params=pltpu.CompilerParams(
            collective_id=0, has_side_effects=True, vmem_limit_bytes=63 * 1024 * 1024
        ),
        name="relay",
    )(
        table,
        inputs.reshape((micro, toks) + block),
        cotangent.reshape((micro, toks) + block),
        norm_gain[0].astype(f32).reshape(block),
        router[0].astype(f32).T.reshape((experts,) + block),
        w_gate[0, 0],
        w_up[0, 0],
        w_down[0, 0],
    )
    return (
        acts.reshape(1, micro, toks, width),
        grads.reshape(1, micro, toks, width),
        rgrad.reshape(experts, width).T[None],
    )


def solution(mesh):
    placed = (
        P(None, ("expert", "dp"), None),
        P(None, ("expert", "dp"), None),
        P("section", None),
        P("section", None, None),
        P("section", "expert", None, "dp"),
        P("section", "expert", None, "dp"),
        P("section", "expert", "dp", None),
        P("section", None, ("expert", "dp"), None),
    )
    return jax.shard_map(
        per_device,
        mesh=mesh,
        in_specs=placed,
        out_specs=(
            P("section", None, ("expert", "dp"), None),
            P("section", None, ("expert", "dp"), None),
            P("section", None, None),
        ),
        check_vma=False,
    )
```

```python
import jax
import jax.numpy as jnp
from jax import lax
from jax.experimental import pallas as pl
from jax.experimental.pallas import tpu as pltpu
from jax.sharding import PartitionSpec as P

EPSILON = 1e-05
MESH = pl.DeviceIdType.MESH
NT = (((1,), (1,)), ((), ()))


def sigmoid(x):
    return jax.nn.sigmoid(x)


def relay_kernel(
    dims,
    table,
    x_in,
    cot_in,
    gain_in,
    router_in,
    wg_hbm,
    wu_hbm,
    wd_hbm,
    acts,
    grads,
    rgrad,
    wg,
    wu,
    wd,
    lin,
    ups,
    hid,
    scl,
    prob,
    pdiff,
    snd,
    disp,
    xf,
    xb,
    gs,
    us,
    act,
    act2,
    obuf,
    osend,
    orecv,
    snd2,
    comb_0,
    comb_1,
    comb_2,
    comb_3,
    racc,
    r1,
    r2,
    r3,
    rsrc,
    w_sem,
    disp_send,
    disp_recv,
    x_send,
    x_recv,
    o_send,
    o_recv,
    comb_send,
    comb_recv,
    hop_send,
    hop_recv,
    r_send,
    r_recv,
):
    n_exp, n_x, cap, toks, chunks, n_ff, n_out, width = dims
    group = n_exp * n_x
    rows = group * cap
    per_x = cap * chunks
    inv_count = 1.0 / (chunks * 128)
    n_group, k_group = xb.shape[1], xb.shape[4]
    group_chunks = k_group // 128
    none = 2 * toks

    section = lax.axis_index("section")
    my_e = lax.axis_index("expert")
    my_dp = lax.axis_index("dp")
    my_x = my_dp // 2
    core = lax.rem(my_dp, 2)
    me = my_e * n_x + my_x

    comb = (comb_0, comb_1, comb_2, comb_3)

    def peer(step):
        q = lax.rem(me + step, group)
        return q, {"expert": q // n_x, "dp": lax.rem(q, n_x) * 2 + core}

    sibling = {"dp": my_x * 2 + 1 - core}
    partner = {"section": 1 - section}

    weights = [
        pltpu.make_async_copy(src, dst, w_sem.at[i])
        for i, (src, dst) in enumerate(((wg_hbm, wg), (wu_hbm, wu), (wd_hbm, wd)))
    ]
    for copy in weights:
        copy.start()

    barrier = pltpu.get_barrier_semaphore()

    @pl.loop(1, group)
    def _(step):
        _, where = peer(step)
        pl.semaphore_signal(barrier, inc=1, device_id=where, device_id_type=MESH)

    @pl.loop(0, n_x)
    def _(x):
        pl.semaphore_signal(
            barrier, inc=1, device_id={"dp": x * 2 + 1 - core}, device_id_type=MESH
        )

    pl.semaphore_signal(barrier, inc=1, device_id=partner, device_id_type=MESH)

    @pl.when(section == 0)
    def _():
        lin[...] = x_in[...]

    @pl.when(section == 1)
    def _():
        ups[...] = cot_in[...]

    hid[:, toks] = jnp.zeros_like(hid[:, toks])
    scl[:, none] = jnp.zeros_like(scl[:, none])
    pl.semaphore_wait(barrier, group + n_x)

    gain = gain_in[...]

    def total(v):
        return jnp.sum(v, axis=(0, 1), keepdims=True)

    def inv_rms_of(v):
        return lax.rsqrt(total(v * v) * inv_count + EPSILON)

    def wait_bytes(ref, sem):
        pltpu.make_async_copy(ref, ref, sem).wait()

    def route(m, t, k):
        return table[m, n_exp * cap + none + 2 * t + k]

    def router_diff(m, t):
        return router_in[route(m, t, 0)] - router_in[route(m, t, 1)]

    def send_dispatch(phase):
        own = pltpu.make_async_copy(snd.at[phase, my_e], disp.at[phase, me], disp_recv.at[phase])
        own.start()

        @pl.loop(1, group)
        def _(step):
            q, where = peer(step)
            pltpu.make_async_remote_copy(
                src_ref=snd.at[phase, q // n_x],
                dst_ref=disp.at[phase, me],
                send_sem=disp_send.at[phase],
                recv_sem=disp_recv.at[phase],
                device_id=where,
                device_id_type=MESH,
            ).start()

    def send_combine(phase):
        own = pltpu.make_async_copy(snd2.at[phase, me], comb[phase].at[me], comb_recv.at[phase])
        own.start()

        @pl.loop(1, group)
        def _(step):
            q, where = peer(step)
            pltpu.make_async_remote_copy(
                src_ref=snd2.at[phase, q],
                dst_ref=comb[phase].at[me],
                send_sem=comb_send.at[phase],
                recv_sem=comb_recv.at[phase],
                device_id=where,
                device_id_type=MESH,
            ).start()

    def hop(ref, dst, which, m):
        return pltpu.make_async_remote_copy(
            src_ref=ref.at[m],
            dst_ref=dst.at[m],
            send_sem=hop_send.at[which, m],
            recv_sem=hop_recv.at[which, m],
            device_id=partner,
            device_id_type=MESH,
        )

    def take_rows(phase):
        wait_bytes(disp.at[phase], disp_recv.at[phase])

        @pl.loop(0, group)
        def _(q):
            block = disp[phase, q].astype(jnp.float32).reshape(per_x, 128)
            xf[pl.ds(pl.multiple_of(q * per_x, 8), per_x), :] = block

        for g in range(n_group):
            for i in range(group_chunks):
                part = xf[pl.ds(g * group_chunks + i, rows, stride=chunks), :]
                xb[phase, g, core, :, i * 128 : (i + 1) * 128] = part.astype(jnp.bfloat16)
            pltpu.make_async_remote_copy(
                src_ref=xb.at[phase, g, core],
                dst_ref=xb.at[phase, g, core],
                send_sem=x_send.at[phase, g],
                recv_sem=x_recv.at[phase, g],
                device_id=sibling,
                device_id_type=MESH,
            ).start()

    def sibling_rows(phase):
        for g in range(n_group):
            wait_bytes(xb.at[phase, g, 1 - core], x_recv.at[phase, g])

    def left(phase, g):
        return xb[phase, g].reshape(2 * rows, k_group)

    def share_tile(phase, n, tile):
        obuf[n] = tile.reshape(2, rows, 256)
        osend[phase, n] = obuf[n, 1 - core].astype(jnp.bfloat16)
        pltpu.make_async_remote_copy(
            src_ref=osend.at[phase, n],
            dst_ref=orecv.at[phase, n],
            send_sem=o_send.at[phase],
            recv_sem=o_recv.at[phase],
            device_id=sibling,
            device_id_type=MESH,
        ).start()

    def give_back(phase):
        wait_bytes(orecv.at[phase], o_recv.at[phase])
        for n in range(n_out):
            both = obuf[n, core] + orecv[phase, n].astype(jnp.float32)
            for i in range(2):
                xf[pl.ds(2 * n + i, rows, stride=chunks), :] = both[:, i * 128 : (i + 1) * 128]

        @pl.loop(0, group)
        def _(q):
            block = xf[pl.ds(pl.multiple_of(q * per_x, 8), per_x), :]
            snd2[phase, q] = block.reshape(cap, chunks, 128).astype(jnp.bfloat16)

        send_combine(phase)

    def fill_slots(phase, m, source, shift):
        for e in range(n_exp):
            for s in range(cap):
                snd[phase, e, s] = source[m, table[m, e * cap + s] >> shift]

    def picked_of(phase, m, t, k):
        slot = table[m, n_exp * cap + 2 * t + k]
        e, s = slot // cap, lax.rem(slot, cap)
        result = comb[phase][e * n_x, s].astype(jnp.float32)
        for x in range(1, n_x):
            result = result + comb[phase][e * n_x + x, s].astype(jnp.float32)
        return result

    def forward_ready(m):
        @pl.when(section == 1)
        def _():
            hop(acts, lin, 0, m).wait_recv()

        for t in range(toks):
            v = lin[m, t].astype(jnp.float32)
            hidden = (v * inv_rms_of(v) * gain).astype(jnp.bfloat16)
            hid[m, t] = hidden
            gap = total(hidden.astype(jnp.float32) * router_diff(m, t))
            prob[m, t, 0] = jnp.broadcast_to(sigmoid(gap), (8, 128))
            prob[m, t, 1] = jnp.broadcast_to(sigmoid(-gap), (8, 128))
        fill_slots(m, m, hid, 1)

    def forward_expert(m):
        sibling_rows(m)
        if m == 0:
            weights[0].wait()
            weights[1].wait()

        @pl.loop(0, n_ff)
        def _(n):
            cols = pl.ds(pl.multiple_of(n * 256, 256), 256)
            gate = jnp.zeros((2 * rows, 256), jnp.float32)
            up = jnp.zeros((2 * rows, 256), jnp.float32)
            for g in range(n_group):
                x = left(m, g)
                k = slice(g * k_group, (g + 1) * k_group)
                gate = gate + jnp.dot(x, wg[k, cols], preferred_element_type=jnp.float32)
                up = up + jnp.dot(x, wu[k, cols], preferred_element_type=jnp.float32)
            gs[m, n] = gate
            us[m, n] = up
            act[n] = (gate * sigmoid(gate) * up).astype(jnp.bfloat16)

        if m == 0:
            weights[2].wait()

        @pl.loop(0, n_out)
        def _(n):
            cols = pl.ds(pl.multiple_of(n * 256, 256), 256)
            tile = jnp.zeros((2 * rows, 256), jnp.float32)
            for k in range(n_ff):
                tile = tile + jnp.dot(
                    act[k], wd[k * 256 : (k + 1) * 256, cols], preferred_element_type=jnp.float32
                )
            share_tile(m, n, tile)

    def forward_end(m):
        wait_bytes(comb[m], comb_recv.at[m])
        for t in range(toks):
            p0 = prob[m, t, 0, 0:1, 0:1]
            p1 = prob[m, t, 1, 0:1, 0:1]
            one, two = picked_of(m, m, t, 0), picked_of(m, m, t, 1)
            v = lin[m, t].astype(jnp.float32)
            acts[m, t] = (v + (p0 * one + p1 * two)).astype(jnp.bfloat16)
            pdiff[m, t] = one - two

        @pl.when(section == 0)
        def _():
            hop(acts, lin, 0, m).start()

    def backward_send(m):
        phase = 2 + m

        @pl.when(section == 0)
        def _():
            hop(grads, ups, 1, m).wait_recv()

        gaps = []
        for t in range(toks):
            up = ups[m, t].astype(jnp.float32)
            p0 = prob[m, t, 0, 0:1, 0:1]
            p1 = prob[m, t, 1, 0:1, 0:1]
            d_gap = p0 * p1 * total(up * pdiff[m, t])
            prob[m, t, 2] = jnp.broadcast_to(d_gap, (8, 128))
            gaps.append(d_gap)
            scl[m, 2 * t] = (p0 * up).astype(jnp.bfloat16)
            scl[m, 2 * t + 1] = (p1 * up).astype(jnp.bfloat16)
        fill_slots(phase, m, scl, 0)
        send_dispatch(phase)
        for e in range(n_exp):
            term = racc[e] if m else jnp.zeros((chunks, 128), jnp.float32)
            for t in range(toks):
                sign = jnp.where(route(m, t, 0) == e, 1.0, 0.0) - jnp.where(
                    route(m, t, 1) == e, 1.0, 0.0
                )
                term = term + (gaps[t] * sign) * hid[m, t].astype(jnp.float32)
            racc[e] = term
        if m:
            router_one()

    def router_one():
        pltpu.make_async_copy(racc.at[my_e], r1.at[my_e], r_recv.at[0]).start()

        @pl.loop(1, n_exp)
        def _(step):
            e = lax.rem(my_e + step, n_exp)
            pltpu.make_async_remote_copy(
                src_ref=racc.at[e],
                dst_ref=r1.at[my_e],
                send_sem=r_send.at[0],
                recv_sem=r_recv.at[0],
                device_id={"expert": e},
                device_id_type=MESH,
            ).start()

    def router_two():
        wait_bytes(r1, r_recv.at[0])
        rsrc[0] = jnp.sum(r1[...], axis=0)
        pltpu.make_async_copy(rsrc.at[0], r2.at[my_dp], r_recv.at[1]).start()

        @pl.loop(1, 2 * n_x)
        def _(step):
            dp = lax.rem(my_dp + step, 2 * n_x)
            pltpu.make_async_remote_copy(
                src_ref=rsrc.at[0],
                dst_ref=r2.at[my_dp],
                send_sem=r_send.at[1],
                recv_sem=r_recv.at[1],
                device_id={"dp": dp},
                device_id_type=MESH,
            ).start()

    def router_three():
        wait_bytes(r2, r_recv.at[1])
        rsrc[1] = jnp.sum(r2[...], axis=0)
        pltpu.make_async_copy(rsrc.at[1], r3.at[my_e], r_recv.at[2]).start()

        @pl.loop(1, n_exp)
        def _(step):
            e = lax.rem(my_e + step, n_exp)
            pltpu.make_async_remote_copy(
                src_ref=rsrc.at[1],
                dst_ref=r3.at[my_e],
                send_sem=r_send.at[2],
                recv_sem=r_recv.at[2],
                device_id={"expert": e},
                device_id_type=MESH,
            ).start()

    def backward_expert(m):
        phase = 2 + m
        sibling_rows(phase)

        @pl.loop(0, n_ff)
        def _(n):
            part = pl.ds(pl.multiple_of(n * 256, 256), 256)
            d_act = jnp.zeros((2 * rows, 256), jnp.float32)
            for g in range(n_group):
                d_act = d_act + lax.dot_general(
                    left(phase, g),
                    wd[part, g * k_group : (g + 1) * k_group],
                    NT,
                    preferred_element_type=jnp.float32,
                )
            gate, up = gs[m, n], us[m, n]
            sig = sigmoid(gate)
            act[n] = (d_act * up * sig * (1.0 + gate * (1.0 - sig))).astype(jnp.bfloat16)
            act2[n] = (d_act * gate * sig).astype(jnp.bfloat16)

        if m:
            router_two()

        @pl.loop(0, n_out)
        def _(n):
            part = pl.ds(pl.multiple_of(n * 256, 256), 256)
            tile = jnp.zeros((2 * rows, 256), jnp.float32)
            for k in range(n_ff):
                cols = slice(k * 256, (k + 1) * 256)
                tile = tile + lax.dot_general(
                    act[k], wg[part, cols], NT, preferred_element_type=jnp.float32
                )
                tile = tile + lax.dot_general(
                    act2[k], wu[part, cols], NT, preferred_element_type=jnp.float32
                )
            share_tile(phase, n, tile)

    def backward_end(m):
        phase = 2 + m
        wait_bytes(comb[phase], comb_recv.at[phase])
        for t in range(toks):
            d_gap = prob[m, t, 2, 0:1, 0:1]
            d_hidden = picked_of(phase, m, t, 0) + picked_of(phase, m, t, 1)
            d_hidden = d_hidden + d_gap * router_diff(m, t)
            v = lin[m, t].astype(jnp.float32)
            up = ups[m, t].astype(jnp.float32)
            inv_rms = inv_rms_of(v)
            weighted = gain * d_hidden
            mean = total(v * weighted) * inv_count
            d_in = up + inv_rms * weighted - v * (inv_rms * inv_rms * inv_rms) * mean
            grads[m, t] = d_in.astype(jnp.bfloat16)

        @pl.when(section == 1)
        def _():
            hop(grads, ups, 1, m).start()

    @pl.when(section == 0)
    def _():
        forward_ready(0)
        send_dispatch(0)
        forward_ready(1)
        take_rows(0)
        send_dispatch(1)
        forward_expert(0)
        give_back(0)
        take_rows(1)
        forward_expert(1)
        forward_end(0)
        give_back(1)
        forward_end(1)
        backward_send(0)
        take_rows(2)
        backward_send(1)
        backward_expert(0)
        give_back(2)
        take_rows(3)
        backward_expert(1)
        give_back(3)
        router_three()
        backward_end(0)
        backward_end(1)

    @pl.when(section == 1)
    def _():
        forward_ready(0)
        send_dispatch(0)
        take_rows(0)
        forward_ready(1)
        send_dispatch(1)
        forward_expert(0)
        give_back(0)
        take_rows(1)
        forward_expert(1)
        give_back(1)
        forward_end(0)
        backward_send(0)
        forward_end(1)
        backward_send(1)
        take_rows(2)
        backward_expert(0)
        give_back(2)
        take_rows(3)
        backward_expert(1)
        backward_end(0)
        give_back(3)
        router_three()
        backward_end(1)

    wait_bytes(r3, r_recv.at[2])
    rgrad[...] = r3[...]

    for phase in range(4):
        wait_bytes(disp.at[phase, pl.ds(0, group - 1)], disp_send.at[phase])
        wait_bytes(comb[phase].at[pl.ds(0, group - 1)], comb_send.at[phase])
        for g in range(n_group):
            wait_bytes(xb.at[phase, g, core], x_send.at[phase, g])
        wait_bytes(osend.at[phase], o_send.at[phase])
    wait_bytes(r1.at[pl.ds(0, n_exp - 1)], r_send.at[0])
    wait_bytes(r2.at[pl.ds(0, 2 * n_x - 1)], r_send.at[1])
    wait_bytes(r1.at[pl.ds(0, n_exp - 1)], r_send.at[2])
    for m in range(2):

        @pl.when(section == 0)
        def _():
            hop(acts, lin, 0, m).wait_send()

        @pl.when(section == 1)
        def _():
            hop(grads, ups, 1, m).wait_send()


def slot_tables(picks, cap, experts):
    micro, toks, top = picks.shape
    flat = picks.reshape(micro, toks * top)
    order = jnp.arange(toks * top, dtype=jnp.int32)
    same = (flat[:, :, None] == flat[:, None, :]) & (order[None, None, :] < order[None, :, None])
    slot_of = flat * cap + jnp.sum(same.astype(jnp.int32), axis=2)
    slots = jnp.arange(experts * cap, dtype=jnp.int32)
    hit = slot_of[:, None, :] == slots[None, :, None]
    gap = toks * top - order
    slot_src = toks * top - jnp.sum(jnp.where(hit, gap[None, None, :], 0), axis=2)
    return jnp.concatenate([slot_src, slot_of, flat], axis=1).astype(jnp.int32)


def per_device(inputs, cotangent, norm_gain, router, w_gate, w_up, w_down, routes):
    micro, toks, width = inputs.shape
    experts = router.shape[2]
    dp = lax.axis_size("dp")
    n_exp, n_x = lax.axis_size("expert"), dp // 2
    cap = 3
    chunks = width // 128
    hidden_units = w_gate.shape[3]
    n_ff, n_out = hidden_units // 256, width // 256
    group = n_exp * n_x
    rows = group * cap
    n_group = 4
    k_group = width // n_group
    table = slot_tables(routes[0], cap, experts)
    bf, f32 = jnp.bfloat16, jnp.float32
    block = (chunks, 128)
    dma = pltpu.SemaphoreType.DMA
    scratch = [
        pltpu.VMEM((width, hidden_units), bf),
        pltpu.VMEM((width, hidden_units), bf),
        pltpu.VMEM((hidden_units, width), bf),
        pltpu.VMEM((micro, toks) + block, bf),
        pltpu.VMEM((micro, toks) + block, bf),
        pltpu.VMEM((micro, toks + 1) + block, bf),
        pltpu.VMEM((micro, 2 * toks + 1) + block, bf),
        pltpu.VMEM((micro, toks, 3, 8, 128), f32),
        pltpu.VMEM((micro, toks) + block, f32),
        pltpu.VMEM((4, n_exp, cap) + block, bf),
        pltpu.VMEM((4, group, cap) + block, bf),
        pltpu.VMEM((rows * chunks, 128), f32),
        pltpu.VMEM((4, n_group, 2, rows, k_group), bf),
        pltpu.VMEM((micro, n_ff, 2 * rows, 256), f32),
        pltpu.VMEM((micro, n_ff, 2 * rows, 256), f32),
        pltpu.VMEM((n_ff, 2 * rows, 256), bf),
        pltpu.VMEM((n_ff, 2 * rows, 256), bf),
        pltpu.VMEM((n_out, 2, rows, 256), f32),
        pltpu.VMEM((4, n_out, rows, 256), bf),
        pltpu.VMEM((4, n_out, rows, 256), bf),
        pltpu.VMEM((4, group, cap) + block, bf),
        pltpu.VMEM((group, cap) + block, bf),
        pltpu.VMEM((group, cap) + block, bf),
        pltpu.VMEM((group, cap) + block, bf),
        pltpu.VMEM((group, cap) + block, bf),
        pltpu.VMEM((n_exp,) + block, f32),
        pltpu.VMEM((n_exp,) + block, f32),
        pltpu.VMEM((dp,) + block, f32),
        pltpu.VMEM((n_exp,) + block, f32),
        pltpu.VMEM((2,) + block, f32),
        dma((3,)),
        dma((4,)),
        dma((4,)),
        dma((4, n_group)),
        dma((4, n_group)),
        dma((4,)),
        dma((4,)),
        dma((4,)),
        dma((4,)),
        dma((2, micro)),
        dma((2, micro)),
        dma((3,)),
        dma((3,)),
    ]
    dims = (n_exp, n_x, cap, toks, chunks, n_ff, n_out, width)
    vmem = pl.BlockSpec(memory_space=pltpu.VMEM)
    hbm = pl.BlockSpec(memory_space=pl.ANY)
    acts, grads, rgrad = pl.pallas_call(
        lambda *refs: relay_kernel(dims, *refs),
        out_shape=(
            jax.ShapeDtypeStruct((micro, toks) + block, bf),
            jax.ShapeDtypeStruct((micro, toks) + block, bf),
            jax.ShapeDtypeStruct((experts,) + block, f32),
        ),
        in_specs=[pl.BlockSpec(memory_space=pltpu.SMEM)] + [vmem] * 4 + [hbm] * 3,
        out_specs=(vmem, vmem, vmem),
        scratch_shapes=scratch,
        compiler_params=pltpu.CompilerParams(
            collective_id=0, has_side_effects=True, vmem_limit_bytes=63 * 1024 * 1024
        ),
        name="relay",
    )(
        table,
        inputs.reshape((micro, toks) + block),
        cotangent.reshape((micro, toks) + block),
        norm_gain[0].astype(f32).reshape(block),
        router[0].astype(f32).T.reshape((experts,) + block),
        w_gate[0, 0],
        w_up[0, 0],
        w_down[0, 0],
    )
    return (
        acts.reshape(1, micro, toks, width),
        grads.reshape(1, micro, toks, width),
        rgrad.reshape(experts, width).T[None],
    )


def solution(mesh):
    placed = (
        P(None, ("expert", "dp"), None),
        P(None, ("expert", "dp"), None),
        P("section", None),
        P("section", None, None),
        P("section", "expert", None, "dp"),
        P("section", "expert", None, "dp"),
        P("section", "expert", "dp", None),
        P("section", None, ("expert", "dp"), None),
    )
    return jax.shard_map(
        per_device,
        mesh=mesh,
        in_specs=placed,
        out_specs=(
            P("section", None, ("expert", "dp"), None),
            P("section", None, ("expert", "dp"), None),
            P("section", None, None),
        ),
        check_vma=False,
    )
```

```python
import jax
import jax.numpy as jnp
from jax import lax
from jax.experimental import pallas as pl
from jax.experimental.pallas import tpu as pltpu
from jax.sharding import PartitionSpec as P

EPSILON = 1e-05
TILE_FF = 512
TILE_OUT = 512
MESH = pl.DeviceIdType.MESH
NT = (((1,), (1,)), ((), ()))


def sigmoid(x):
    return jax.nn.sigmoid(x)


def relay_kernel(
    dims,
    table,
    x_in,
    cot_in,
    gain_in,
    router_in,
    wg_hbm,
    wu_hbm,
    wd_hbm,
    acts_out,
    grads_out,
    rgrad,
    wg,
    wu,
    wd,
    acts,
    grads,
    gain_f,
    router_f,
    flat,
    lin,
    ups,
    hid,
    scl,
    prob,
    pdiff,
    snd,
    disp,
    xf,
    xb,
    gs,
    us,
    act,
    act2,
    obuf,
    osend,
    orecv,
    snd2_early,
    snd2_late,
    early_0,
    early_1,
    early_2,
    early_3,
    late_0,
    late_1,
    late_2,
    late_3,
    racc,
    r1,
    r2,
    r3,
    rsrc,
    w_sem,
    disp_send,
    disp_recv,
    x_send,
    x_recv,
    o_send,
    o_recv,
    comb_send,
    comb_recv,
    hop_send,
    hop_recv,
    r_send,
    r_recv,
):
    n_exp, n_x, cap, toks, chunks, n_ff, n_out, n_early, n_batch, tile_ff, tile_out = dims
    group = n_exp * n_x
    rows = group * cap
    per_x = cap * chunks
    inv_count = 1.0 / (chunks * 128)
    batch = group // n_batch
    none = 2 * toks

    section = lax.axis_index("section")
    my_e = lax.axis_index("expert")
    my_dp = lax.axis_index("dp")
    my_x = my_dp // 2
    core = lax.rem(my_dp, 2)
    me = my_e * n_x + my_x

    comb = ((early_0, late_0), (early_1, late_1), (early_2, late_2), (early_3, late_3))
    snd2 = (snd2_early, snd2_late)
    tile_chunks = tile_out // 128
    starts, stops = (0, n_early), (n_early, n_out)

    def peer(step):
        q = lax.rem(me + step, group)
        return q, {"expert": q // n_x, "dp": lax.rem(q, n_x) * 2 + core}

    sibling = {"dp": my_x * 2 + 1 - core}
    partner = {"section": 1 - section}

    weights = [
        pltpu.make_async_copy(src, dst, w_sem.at[i])
        for i, (src, dst) in enumerate(((wg_hbm, wg), (wu_hbm, wu), (wd_hbm, wd)))
    ]
    for copy in weights:
        copy.start()

    barrier = pltpu.get_barrier_semaphore()

    @pl.loop(1, group)
    def _(step):
        _, where = peer(step)
        pl.semaphore_signal(barrier, inc=1, device_id=where, device_id_type=MESH)

    @pl.loop(0, n_x)
    def _(x):
        pl.semaphore_signal(
            barrier, inc=1, device_id={"dp": x * 2 + 1 - core}, device_id_type=MESH
        )

    pl.semaphore_signal(barrier, inc=1, device_id=partner, device_id_type=MESH)

    def rows_to_blocks(source, target):
        for m in range(2):
            for j in range(chunks):
                piece = source[m, :, j * 128 : (j + 1) * 128]
                flat[j * toks : (j + 1) * toks, :] = piece.astype(jnp.float32)
            for t in range(toks):
                target[m, t] = flat[pl.ds(t, chunks, stride=toks), :].astype(jnp.bfloat16)

    def blocks_to_rows(source, target, m):
        for t in range(toks):
            flat[pl.ds(t, chunks, stride=toks), :] = source[m, t].astype(jnp.float32)
        for j in range(chunks):
            piece = flat[j * toks : (j + 1) * toks, :]
            target[m, :, j * 128 : (j + 1) * 128] = piece.astype(jnp.bfloat16)

    @pl.when(section == 0)
    def _():
        rows_to_blocks(x_in, lin)

    @pl.when(section == 1)
    def _():
        rows_to_blocks(cot_in, ups)

    for j in range(chunks):
        gain_f[j : j + 1, :] = gain_in[0:1, j * 128 : (j + 1) * 128].astype(jnp.float32)
    for j in range(chunks):
        piece = router_in[:, j * 128 : (j + 1) * 128]
        flat[j * n_exp : (j + 1) * n_exp, :] = piece.astype(jnp.float32)
    for e in range(n_exp):
        router_f[e] = flat[pl.ds(e, chunks, stride=n_exp), :]

    hid[:, toks] = jnp.zeros_like(hid[:, toks])
    scl[:, none] = jnp.zeros_like(scl[:, none])
    gain = gain_f[...]

    def total(v):
        return jnp.sum(v, axis=(0, 1), keepdims=True)

    def inv_rms_of(v):
        return lax.rsqrt(total(v * v) * inv_count + EPSILON)

    def wait_bytes(ref, sem):
        pltpu.make_async_copy(ref, ref, sem).wait()

    def route(m, t, k):
        return table[m, n_exp * cap + none + 2 * t + k]

    def router_diff(m, t):
        return router_f[route(m, t, 0)] - router_f[route(m, t, 1)]

    def each_step(body):
        for step in range(1, 4):
            body(step)

        @pl.loop(1, group // 4)
        def _(turn):
            for part in range(4):
                body(turn * 4 + part)

    def send_dispatch(phase):
        pltpu.make_async_copy(
            snd.at[phase, my_e], disp.at[phase, core, 0], disp_recv.at[phase, 0]
        ).start()

        def send(step):
            q, where = peer(step)
            pltpu.make_async_remote_copy(
                src_ref=snd.at[phase, q // n_x],
                dst_ref=disp.at[phase, core, step],
                send_sem=disp_send.at[phase],
                recv_sem=disp_recv.at[phase, step // batch],
                device_id=where,
                device_id_type=MESH,
            ).start()

        each_step(send)

    def send_combine(phase, part):
        pltpu.make_async_copy(
            snd2[part].at[phase, 0], comb[phase][part].at[me], comb_recv.at[phase, part]
        ).start()

        def send(step):
            _, where = peer(group - step)
            pltpu.make_async_remote_copy(
                src_ref=snd2[part].at[phase, step],
                dst_ref=comb[phase][part].at[me],
                send_sem=comb_send.at[phase, part],
                recv_sem=comb_recv.at[phase, part],
                device_id=where,
                device_id_type=MESH,
            ).start()

        each_step(send)

    def hop(ref, dst, which, m):
        return pltpu.make_async_remote_copy(
            src_ref=ref.at[m],
            dst_ref=dst.at[m],
            send_sem=hop_send.at[which, m],
            recv_sem=hop_recv.at[which, m],
            device_id=partner,
            device_id_type=MESH,
        )

    def batch_of(phase, half, b):
        return disp.at[phase, half, pl.ds(b * batch, batch)]

    def unpack(phase, half, b):
        @pl.loop(b * batch, (b + 1) * batch)
        def _(q):
            block = disp[phase, half, q].astype(jnp.float32).reshape(per_x, 128)
            xf[pl.ds(pl.multiple_of(q * per_x, 8), per_x), :] = block

    def to_rows(half):
        for j in range(chunks):
            part = xf[pl.ds(j, rows, stride=chunks), :]
            xb[half, :, j * 128 : (j + 1) * 128] = part.astype(jnp.bfloat16)

    def take_rows(phase):
        for b in range(n_batch):
            wait_bytes(batch_of(phase, core, b), disp_recv.at[phase, b])
            pltpu.make_async_remote_copy(
                src_ref=batch_of(phase, core, b),
                dst_ref=batch_of(phase, core, b),
                send_sem=x_send.at[phase],
                recv_sem=x_recv.at[phase, b],
                device_id=sibling,
                device_id_type=MESH,
            ).start()
            unpack(phase, core, b)
        to_rows(core)

    def sibling_rows(phase):
        for b in range(n_batch):
            wait_bytes(batch_of(phase, 1 - core, b), x_recv.at[phase, b])
            unpack(phase, 1 - core, b)
        to_rows(1 - core)

    def left():
        return xb[...].reshape(2 * rows, chunks * 128)

    def share_tile(phase, n, tile):
        obuf[n] = tile.reshape(2, rows, tile_out)
        osend[phase, n] = obuf[n, 1 - core].astype(jnp.bfloat16)
        pltpu.make_async_remote_copy(
            src_ref=osend.at[phase, n],
            dst_ref=orecv.at[phase, n],
            send_sem=o_send.at[phase],
            recv_sem=o_recv.at[phase, n // n_early],
            device_id=sibling,
            device_id_type=MESH,
        ).start()

    def give_back(phase, part=1):
        first, last = starts[part], stops[part]
        span = (last - first) * tile_chunks
        wait_bytes(orecv.at[phase, pl.ds(first, last - first)], o_recv.at[phase, part])
        for n in range(first, last):
            both = obuf[n, core] + orecv[phase, n].astype(jnp.float32)
            for i in range(tile_chunks):
                at = (n - first) * tile_chunks + i
                xf[pl.ds(at, rows, stride=span), :] = both[:, i * 128 : (i + 1) * 128]

        @pl.loop(0, group)
        def _(q):
            size = cap * span
            block = xf[pl.ds(pl.multiple_of(q * size, 8), size), :]
            snd2[part][phase, q] = block.reshape(cap, span, 128).astype(jnp.bfloat16)

        send_combine(phase, part)

    def over_tiles(phase, body):
        pl.loop(0, min(n_early + 1, n_out))(body)
        give_back(phase, 0)
        if n_early + 1 < n_out:
            pl.loop(n_early + 1, n_out)(body)

    def await_combine(phase):
        for part in range(2):
            wait_bytes(comb[phase][part], comb_recv.at[phase, part])

    def fill_slots(phase, m, source, shift):
        for e in range(n_exp):
            for s in range(cap):
                snd[phase, e, s] = source[m, table[m, e * cap + s] >> shift]

    def picked_of(phase, m, t, k):
        slot = table[m, n_exp * cap + 2 * t + k]
        e, s = slot // cap, lax.rem(slot, cap)
        parts = []
        for ref in comb[phase]:
            result = ref[e * n_x, s].astype(jnp.float32)
            for x in range(1, n_x):
                result = result + ref[e * n_x + x, s].astype(jnp.float32)
            parts.append(result)
        return jnp.concatenate(parts, axis=0)

    def forward_ready(m):
        @pl.when(section == 1)
        def _():
            hop(acts, lin, 0, m).wait_recv()

        for t in range(toks):
            v = lin[m, t].astype(jnp.float32)
            hidden = (v * inv_rms_of(v) * gain).astype(jnp.bfloat16)
            hid[m, t] = hidden
            gap = total(hidden.astype(jnp.float32) * router_diff(m, t))
            prob[m, t, 0] = jnp.broadcast_to(sigmoid(gap), (8, 128))
            prob[m, t, 1] = jnp.broadcast_to(sigmoid(-gap), (8, 128))
        fill_slots(m, m, hid, 1)

    def forward_expert(m):
        sibling_rows(m)
        if m == 0:
            weights[0].wait()
            weights[1].wait()

        @pl.loop(0, n_ff)
        def _(n):
            cols = pl.ds(pl.multiple_of(n * tile_ff, tile_ff), tile_ff)
            gate = jnp.dot(left(), wg[:, cols], preferred_element_type=jnp.float32)
            gs[m, n] = gate
            up = jnp.dot(left(), wu[:, cols], preferred_element_type=jnp.float32)
            us[m, n] = up
            act[:, cols] = (gate * sigmoid(gate) * up).astype(jnp.bfloat16)

        if m == 0:
            weights[2].wait()

        def out_tile(n):
            cols = pl.ds(pl.multiple_of(n * tile_out, tile_out), tile_out)
            tile = jnp.dot(act[...], wd[:, cols], preferred_element_type=jnp.float32)
            share_tile(m, n, tile)

        over_tiles(m, out_tile)

    def forward_end(m):
        await_combine(m)
        for t in range(toks):
            p0 = prob[m, t, 0, 0:1, 0:1]
            p1 = prob[m, t, 1, 0:1, 0:1]
            one, two = picked_of(m, m, t, 0), picked_of(m, m, t, 1)
            v = lin[m, t].astype(jnp.float32)
            acts[m, t] = (v + (p0 * one + p1 * two)).astype(jnp.bfloat16)
            pdiff[m, t] = one - two

        @pl.when(section == 0)
        def _():
            hop(acts, lin, 0, m).start()

        blocks_to_rows(acts, acts_out, m)

    def backward_send(m):
        phase = 2 + m

        @pl.when(section == 0)
        def _():
            hop(grads, ups, 1, m).wait_recv()

        gaps = []
        for t in range(toks):
            up = ups[m, t].astype(jnp.float32)
            p0 = prob[m, t, 0, 0:1, 0:1]
            p1 = prob[m, t, 1, 0:1, 0:1]
            d_gap = p0 * p1 * total(up * pdiff[m, t])
            prob[m, t, 2] = jnp.broadcast_to(d_gap, (8, 128))
            gaps.append(d_gap)
            scl[m, 2 * t] = (p0 * up).astype(jnp.bfloat16)
            scl[m, 2 * t + 1] = (p1 * up).astype(jnp.bfloat16)
        fill_slots(phase, m, scl, 0)
        send_dispatch(phase)
        for e in range(n_exp):
            term = racc[e] if m else jnp.zeros((chunks, 128), jnp.float32)
            for t in range(toks):
                sign = jnp.where(route(m, t, 0) == e, 1.0, 0.0) - jnp.where(
                    route(m, t, 1) == e, 1.0, 0.0
                )
                term = term + (gaps[t] * sign) * hid[m, t].astype(jnp.float32)
            racc[e] = term
        if m:
            router_one()

    def router_one():
        pltpu.make_async_copy(racc.at[my_e], r1.at[my_e], r_recv.at[0]).start()

        @pl.loop(1, n_exp)
        def _(step):
            e = lax.rem(my_e + step, n_exp)
            pltpu.make_async_remote_copy(
                src_ref=racc.at[e],
                dst_ref=r1.at[my_e],
                send_sem=r_send.at[0],
                recv_sem=r_recv.at[0],
                device_id={"expert": e},
                device_id_type=MESH,
            ).start()

    def router_two():
        wait_bytes(r1, r_recv.at[0])
        rsrc[0] = jnp.sum(r1[...], axis=0)
        pltpu.make_async_copy(rsrc.at[0], r2.at[my_dp], r_recv.at[1]).start()

        @pl.loop(1, 2 * n_x)
        def _(step):
            dp = lax.rem(my_dp + step, 2 * n_x)
            pltpu.make_async_remote_copy(
                src_ref=rsrc.at[0],
                dst_ref=r2.at[my_dp],
                send_sem=r_send.at[1],
                recv_sem=r_recv.at[1],
                device_id={"dp": dp},
                device_id_type=MESH,
            ).start()

    def router_three():
        wait_bytes(r2, r_recv.at[1])
        rsrc[1] = jnp.sum(r2[...], axis=0)
        pltpu.make_async_copy(rsrc.at[1], r3.at[my_e], r_recv.at[2]).start()

        @pl.loop(1, n_exp)
        def _(step):
            e = lax.rem(my_e + step, n_exp)
            pltpu.make_async_remote_copy(
                src_ref=rsrc.at[1],
                dst_ref=r3.at[my_e],
                send_sem=r_send.at[2],
                recv_sem=r_recv.at[2],
                device_id={"expert": e},
                device_id_type=MESH,
            ).start()

    def backward_expert(m):
        phase = 2 + m
        sibling_rows(phase)

        @pl.loop(0, n_ff)
        def _(n):
            part = pl.ds(pl.multiple_of(n * tile_ff, tile_ff), tile_ff)
            d_act = lax.dot_general(
                left(), wd[part, :], NT, preferred_element_type=jnp.float32
            )
            gate, up = gs[m, n], us[m, n]
            sig = sigmoid(gate)
            act[:, part] = (d_act * up * sig * (1.0 + gate * (1.0 - sig))).astype(jnp.bfloat16)
            act2[:, part] = (d_act * gate * sig).astype(jnp.bfloat16)

        if m:
            router_two()

        def back_tile(n):
            part = pl.ds(pl.multiple_of(n * tile_out, tile_out), tile_out)
            tile = lax.dot_general(act[...], wg[part, :], NT, preferred_element_type=jnp.float32)
            tile = tile + lax.dot_general(
                act2[...], wu[part, :], NT, preferred_element_type=jnp.float32
            )
            share_tile(phase, n, tile)

        over_tiles(phase, back_tile)

    def backward_end(m):
        phase = 2 + m
        await_combine(phase)
        for t in range(toks):
            d_gap = prob[m, t, 2, 0:1, 0:1]
            d_hidden = picked_of(phase, m, t, 0) + picked_of(phase, m, t, 1)
            d_hidden = d_hidden + d_gap * router_diff(m, t)
            v = lin[m, t].astype(jnp.float32)
            up = ups[m, t].astype(jnp.float32)
            inv_rms = inv_rms_of(v)
            weighted = gain * d_hidden
            mean = total(v * weighted) * inv_count
            d_in = up + inv_rms * weighted - v * (inv_rms * inv_rms * inv_rms) * mean
            grads[m, t] = d_in.astype(jnp.bfloat16)

        @pl.when(section == 1)
        def _():
            hop(grads, ups, 1, m).start()

        blocks_to_rows(grads, grads_out, m)

    @pl.when(section == 0)
    def _():
        forward_ready(0)

    pl.semaphore_wait(barrier, group + n_x)

    @pl.when(section == 0)
    def _():
        send_dispatch(0)
        forward_ready(1)
        take_rows(0)
        send_dispatch(1)
        forward_expert(0)
        give_back(0)
        take_rows(1)
        forward_expert(1)
        forward_end(0)
        give_back(1)
        forward_end(1)
        backward_send(0)
        take_rows(2)
        backward_send(1)
        backward_expert(0)
        give_back(2)
        take_rows(3)
        backward_expert(1)
        give_back(3)
        router_three()
        backward_end(0)
        backward_end(1)

    @pl.when(section == 1)
    def _():
        forward_ready(0)
        send_dispatch(0)
        take_rows(0)
        forward_ready(1)
        send_dispatch(1)
        forward_expert(0)
        give_back(0)
        take_rows(1)
        forward_expert(1)
        give_back(1)
        forward_end(0)
        backward_send(0)
        forward_end(1)
        backward_send(1)
        take_rows(2)
        backward_expert(0)
        give_back(2)
        take_rows(3)
        backward_expert(1)
        backward_end(0)
        give_back(3)
        router_three()
        backward_end(1)

    wait_bytes(r3, r_recv.at[2])
    for e in range(n_exp):
        flat[pl.ds(e, chunks, stride=n_exp), :] = r3[e]
    for j in range(chunks):
        rgrad[:, j * 128 : (j + 1) * 128] = flat[j * n_exp : (j + 1) * n_exp, :]

    for phase in range(4):
        wait_bytes(disp.at[phase, core, pl.ds(0, group - 1)], disp_send.at[phase])
        for part in range(2):
            sent = comb[phase][part].at[pl.ds(0, group - 1)]
            wait_bytes(sent, comb_send.at[phase, part])
        wait_bytes(disp.at[phase, core], x_send.at[phase])
        wait_bytes(osend.at[phase], o_send.at[phase])
    wait_bytes(r1.at[pl.ds(0, n_exp - 1)], r_send.at[0])
    wait_bytes(r2.at[pl.ds(0, 2 * n_x - 1)], r_send.at[1])
    wait_bytes(r1.at[pl.ds(0, n_exp - 1)], r_send.at[2])
    for m in range(2):

        @pl.when(section == 0)
        def _():
            hop(acts, lin, 0, m).wait_send()

        @pl.when(section == 1)
        def _():
            hop(grads, ups, 1, m).wait_send()


def finish_kernel(acts, grads, rgrad, acts_out, grads_out, rgrad_out):
    acts_out[...] = acts[...]
    grads_out[...] = grads[...]
    rgrad_out[...] = rgrad[...]


def slot_tables(picks, cap, experts):
    micro, toks, top = picks.shape
    flat = picks.reshape(micro, toks * top)
    order = jnp.arange(toks * top, dtype=jnp.int32)
    same = (flat[:, :, None] == flat[:, None, :]) & (order[None, None, :] < order[None, :, None])
    slot_of = flat * cap + jnp.sum(same.astype(jnp.int32), axis=2)
    slots = jnp.arange(experts * cap, dtype=jnp.int32)
    hit = slot_of[:, None, :] == slots[None, :, None]
    gap = toks * top - order
    slot_src = toks * top - jnp.sum(jnp.where(hit, gap[None, None, :], 0), axis=2)
    return jnp.concatenate([slot_src, slot_of, flat], axis=1).astype(jnp.int32)


def per_device(inputs, cotangent, norm_gain, router, w_gate, w_up, w_down, routes):
    micro, toks, width = inputs.shape
    experts = router.shape[2]
    dp = lax.axis_size("dp")
    n_exp, n_x = lax.axis_size("expert"), dp // 2
    cap = 3
    chunks = width // 128
    hidden_units = w_gate.shape[3]
    tile_ff, tile_out = min(TILE_FF, hidden_units), min(TILE_OUT, width)
    n_ff, n_out = hidden_units // tile_ff, width // tile_out
    group = n_exp * n_x
    rows = group * cap
    n_batch = 4
    table = slot_tables(routes[0], cap, experts)
    bf, f32 = jnp.bfloat16, jnp.float32
    block = (chunks, 128)
    n_early = max(n_out * 2 // 3, 1)
    early = (n_early * tile_out // 128, 128)
    late = ((n_out - n_early) * tile_out // 128, 128)
    dma = pltpu.SemaphoreType.DMA
    scratch = [
        pltpu.VMEM((width, hidden_units), bf),
        pltpu.VMEM((width, hidden_units), bf),
        pltpu.VMEM((hidden_units, width), bf),
        pltpu.VMEM((micro, toks) + block, bf),
        pltpu.VMEM((micro, toks) + block, bf),
        pltpu.VMEM(block, f32),
        pltpu.VMEM((experts,) + block, f32),
        pltpu.VMEM((chunks * 8, 128), f32),
        pltpu.VMEM((micro, toks) + block, bf),
        pltpu.VMEM((micro, toks) + block, bf),
        pltpu.VMEM((micro, toks + 1) + block, bf),
        pltpu.VMEM((micro, 2 * toks + 1) + block, bf),
        pltpu.VMEM((micro, toks, 3, 8, 128), f32),
        pltpu.VMEM((micro, toks) + block, f32),
        pltpu.VMEM((4, n_exp, cap) + block, bf),
        pltpu.VMEM((4, 2, group, cap) + block, bf),
        pltpu.VMEM((rows * chunks, 128), f32),
        pltpu.VMEM((2, rows, width), bf),
        pltpu.VMEM((micro, n_ff, 2 * rows, tile_ff), f32),
        pltpu.VMEM((micro, n_ff, 2 * rows, tile_ff), f32),
        pltpu.VMEM((2 * rows, hidden_units), bf),
        pltpu.VMEM((2 * rows, hidden_units), bf),
        pltpu.VMEM((n_out, 2, rows, tile_out), f32),
        pltpu.VMEM((4, n_out, rows, tile_out), bf),
        pltpu.VMEM((4, n_out, rows, tile_out), bf),
        pltpu.VMEM((4, group, cap) + early, bf),
        pltpu.VMEM((4, group, cap) + late, bf),
        pltpu.VMEM((group, cap) + early, bf),
        pltpu.VMEM((group, cap) + early, bf),
        pltpu.VMEM((group, cap) + early, bf),
        pltpu.VMEM((group, cap) + early, bf),
        pltpu.VMEM((group, cap) + late, bf),
        pltpu.VMEM((group, cap) + late, bf),
        pltpu.VMEM((group, cap) + late, bf),
        pltpu.VMEM((group, cap) + late, bf),
        pltpu.VMEM((n_exp,) + block, f32),
        pltpu.VMEM((n_exp,) + block, f32),
        pltpu.VMEM((dp,) + block, f32),
        pltpu.VMEM((n_exp,) + block, f32),
        pltpu.VMEM((2,) + block, f32),
        dma((3,)),
        dma((4,)),
        dma((4, n_batch)),
        dma((4,)),
        dma((4, n_batch)),
        dma((4,)),
        dma((4, 2)),
        dma((4, 2)),
        dma((4, 2)),
        dma((2, micro)),
        dma((2, micro)),
        dma((3,)),
        dma((3,)),
    ]
    dims = (n_exp, n_x, cap, toks, chunks, n_ff, n_out, n_early, n_batch, tile_ff, tile_out)
    vmem = pl.BlockSpec(memory_space=pltpu.VMEM)
    hbm = pl.BlockSpec(memory_space=pl.ANY)
    acts, grads, rgrad = pl.pallas_call(
        lambda *refs: relay_kernel(dims, *refs),
        out_shape=(
            jax.ShapeDtypeStruct((micro, toks, width), bf),
            jax.ShapeDtypeStruct((micro, toks, width), bf),
            jax.ShapeDtypeStruct((experts, width), f32),
        ),
        in_specs=[pl.BlockSpec(memory_space=pltpu.SMEM)] + [vmem] * 4 + [hbm] * 3,
        out_specs=(vmem, vmem, vmem),
        scratch_shapes=scratch,
        compiler_params=pltpu.CompilerParams(
            collective_id=0, has_side_effects=True, vmem_limit_bytes=63 * 1024 * 1024
        ),
        name="relay",
    )(
        table,
        inputs,
        cotangent,
        norm_gain,
        router[0].T,
        w_gate[0, 0],
        w_up[0, 0],
        w_down[0, 0],
    )
    acts, grads, rgrad = pl.pallas_call(
        finish_kernel,
        out_shape=tuple(jax.ShapeDtypeStruct(a.shape, a.dtype) for a in (acts, grads, rgrad)),
        in_specs=[vmem] * 3,
        out_specs=(vmem,) * 3,
        name="finish",
    )(acts, grads, rgrad)
    return (
        acts[None],
        grads[None],
        rgrad.T[None],
    )


def solution(mesh):
    placed = (
        P(None, ("expert", "dp"), None),
        P(None, ("expert", "dp"), None),
        P("section", None),
        P("section", None, None),
        P("section", "expert", None, "dp"),
        P("section", "expert", None, "dp"),
        P("section", "expert", "dp", None),
        P("section", None, ("expert", "dp"), None),
    )
    return jax.shard_map(
        per_device,
        mesh=mesh,
        in_specs=placed,
        out_specs=(
            P("section", None, ("expert", "dp"), None),
            P("section", None, ("expert", "dp"), None),
            P("section", None, None),
        ),
        check_vma=False,
    )
```

```python
import jax
import jax.numpy as jnp
from jax import lax
from jax.experimental import pallas as pl
from jax.experimental.pallas import tpu as pltpu
from jax.sharding import PartitionSpec as P

EPSILON = 1e-05
TILE_FF = 512
TILE_OUT = 512
MESH = pl.DeviceIdType.MESH
NT = (((1,), (1,)), ((), ()))


def sigmoid(x):
    return jax.nn.sigmoid(x)


def relay_kernel(
    dims,
    table,
    x_in,
    cot_in,
    gain_in,
    router_in,
    wg_hbm,
    wu_hbm,
    wd_hbm,
    acts_out,
    grads_out,
    rgrad,
    wg,
    wu,
    wd,
    acts,
    grads,
    gain_f,
    router_f,
    flat,
    lin,
    ups,
    hid,
    scl,
    prob,
    pdiff,
    snd,
    disp,
    xf,
    xb,
    gs,
    us,
    act,
    act2,
    obuf,
    osend,
    orecv,
    snd2,
    comb_0,
    comb_1,
    comb_2,
    comb_3,
    racc,
    r1,
    r2,
    r3,
    rsrc,
    w_sem,
    disp_send,
    disp_recv,
    x_send,
    x_recv,
    o_send,
    o_recv,
    comb_send,
    comb_recv,
    hop_send,
    hop_recv,
    r_send,
    r_recv,
):
    n_exp, n_x, cap, toks, chunks, n_ff, n_out, n_early, n_batch, tile_ff, tile_out = dims
    group = n_exp * n_x
    rows = group * cap
    per_x = cap * chunks
    inv_count = 1.0 / (chunks * 128)
    batch = group // n_batch
    none = 2 * toks

    section = lax.axis_index("section")
    my_e = lax.axis_index("expert")
    my_dp = lax.axis_index("dp")
    my_x = my_dp // 2
    core = lax.rem(my_dp, 2)
    me = my_e * n_x + my_x

    comb = (comb_0, comb_1, comb_2, comb_3)
    tile_chunks = tile_out // 128
    halves = ((0, n_early), (n_early, n_out))

    def pieces_of(phase):
        return ((0, n_out),) if phase < 2 else halves

    def span_of(piece):
        return pl.ds(piece[0] * tile_chunks, (piece[1] - piece[0]) * tile_chunks)

    def wrapped(value, size):
        return jnp.where(value >= size, value - size, value)

    ahead = [wrapped(my_x + dx, n_x) * 2 + core for dx in range(n_x)]
    behind = [wrapped(my_x + n_x - dx, n_x) * 2 + core for dx in range(n_x)]

    def each_step(body, back=False):
        columns = behind if back else ahead
        for dx in range(1, n_x):
            body(0, dx, my_e, {"expert": my_e, "dp": columns[dx]})

        @pl.loop(1, n_exp)
        def _(de):
            e = wrapped(my_e + n_exp - de if back else my_e + de, n_exp)
            for dx in range(n_x):
                body(de, dx, e, {"expert": e, "dp": columns[dx]})

    sibling = {"dp": my_x * 2 + 1 - core}
    partner = {"section": 1 - section}

    weights = [
        pltpu.make_async_copy(src, dst, w_sem.at[i])
        for i, (src, dst) in enumerate(((wg_hbm, wg), (wu_hbm, wu), (wd_hbm, wd)))
    ]
    for copy in weights:
        copy.start()

    barrier = pltpu.get_barrier_semaphore()

    def greet(de, dx, e, where):
        pl.semaphore_signal(barrier, inc=1, device_id=where, device_id_type=MESH)

    each_step(greet)

    @pl.loop(0, n_x)
    def _(x):
        pl.semaphore_signal(
            barrier, inc=1, device_id={"dp": x * 2 + 1 - core}, device_id_type=MESH
        )

    pl.semaphore_signal(barrier, inc=1, device_id=partner, device_id_type=MESH)

    def rows_to_blocks(source, target):
        for m in range(2):
            for j in range(chunks):
                piece = source[m, :, j * 128 : (j + 1) * 128]
                flat[j * toks : (j + 1) * toks, :] = piece.astype(jnp.float32)
            for t in range(toks):
                target[m, t] = flat[pl.ds(t, chunks, stride=toks), :].astype(jnp.bfloat16)

    def blocks_to_rows(source, target, m):
        for t in range(toks):
            flat[pl.ds(t, chunks, stride=toks), :] = source[m, t].astype(jnp.float32)
        for j in range(chunks):
            piece = flat[j * toks : (j + 1) * toks, :]
            target[m, :, j * 128 : (j + 1) * 128] = piece.astype(jnp.bfloat16)

    @pl.when(section == 0)
    def _():
        rows_to_blocks(x_in, lin)

    @pl.when(section == 1)
    def _():
        rows_to_blocks(cot_in, ups)

    for j in range(chunks):
        gain_f[j : j + 1, :] = gain_in[0:1, j * 128 : (j + 1) * 128].astype(jnp.float32)
    for j in range(chunks):
        piece = router_in[:, j * 128 : (j + 1) * 128]
        flat[j * n_exp : (j + 1) * n_exp, :] = piece.astype(jnp.float32)
    for e in range(n_exp):
        router_f[e] = flat[pl.ds(e, chunks, stride=n_exp), :]

    hid[:, toks] = jnp.zeros_like(hid[:, toks])
    scl[:, none] = jnp.zeros_like(scl[:, none])
    gain = gain_f[...]

    def total(v):
        return jnp.sum(v, axis=(0, 1), keepdims=True)

    def inv_rms_of(v):
        return lax.rsqrt(total(v * v) * inv_count + EPSILON)

    def wait_bytes(ref, sem):
        pltpu.make_async_copy(ref, ref, sem).wait()

    def route(m, t, k):
        return table[m, n_exp * cap + none + 2 * t + k]

    def router_diff(m, t):
        return router_f[route(m, t, 0)] - router_f[route(m, t, 1)]

    def send_dispatch(phase):
        pltpu.make_async_copy(
            snd.at[phase, my_e], disp.at[phase, core, 0], disp_recv.at[phase, 0]
        ).start()

        def send(de, dx, e, where):
            pltpu.make_async_remote_copy(
                src_ref=snd.at[phase, e],
                dst_ref=disp.at[phase, core, de * n_x + dx],
                send_sem=disp_send.at[phase],
                recv_sem=disp_recv.at[phase, de // (batch // n_x)],
                device_id=where,
                device_id_type=MESH,
            ).start()

        each_step(send)

    def send_combine(phase, part):
        span = span_of(pieces_of(phase)[part])
        pltpu.make_async_copy(
            snd2.at[phase, 0, :, span], comb[phase].at[me, :, span], comb_recv.at[phase, part]
        ).start()

        def send(de, dx, e, where):
            pltpu.make_async_remote_copy(
                src_ref=snd2.at[phase, de * n_x + dx, :, span],
                dst_ref=comb[phase].at[me, :, span],
                send_sem=comb_send.at[phase, part],
                recv_sem=comb_recv.at[phase, part],
                device_id=where,
                device_id_type=MESH,
            ).start()

        each_step(send, back=True)

    def hop(ref, dst, which, m):
        return pltpu.make_async_remote_copy(
            src_ref=ref.at[m],
            dst_ref=dst.at[m],
            send_sem=hop_send.at[which, m],
            recv_sem=hop_recv.at[which, m],
            device_id=partner,
            device_id_type=MESH,
        )

    def batch_of(phase, half, b):
        return disp.at[phase, half, pl.ds(b * batch, batch)]

    def unpack(phase, half, b):
        @pl.loop(b * batch, (b + 1) * batch)
        def _(q):
            block = disp[phase, half, q].astype(jnp.float32).reshape(per_x, 128)
            xf[pl.ds(pl.multiple_of(q * per_x, 8), per_x), :] = block

    def to_rows(half):
        for j in range(chunks):
            part = xf[pl.ds(j, rows, stride=chunks), :]
            xb[half, :, j * 128 : (j + 1) * 128] = part.astype(jnp.bfloat16)

    def take_rows(phase):
        for b in range(n_batch):
            wait_bytes(batch_of(phase, core, b), disp_recv.at[phase, b])
            pltpu.make_async_remote_copy(
                src_ref=batch_of(phase, core, b),
                dst_ref=batch_of(phase, core, b),
                send_sem=x_send.at[phase],
                recv_sem=x_recv.at[phase, b],
                device_id=sibling,
                device_id_type=MESH,
            ).start()
            unpack(phase, core, b)
        to_rows(core)

    def sibling_rows(phase):
        for b in range(n_batch):
            wait_bytes(batch_of(phase, 1 - core, b), x_recv.at[phase, b])
            unpack(phase, 1 - core, b)
        to_rows(1 - core)

    def left():
        return xb[...].reshape(2 * rows, chunks * 128)

    def share_tile(phase, n, tile):
        obuf[n] = tile.reshape(2, rows, tile_out)
        osend[phase, n] = obuf[n, 1 - core].astype(jnp.bfloat16)
        pltpu.make_async_remote_copy(
            src_ref=osend.at[phase, n],
            dst_ref=orecv.at[phase, n],
            send_sem=o_send.at[phase],
            recv_sem=o_recv.at[phase, n // n_early],
            device_id=sibling,
            device_id_type=MESH,
        ).start()

    def give_back(phase, part):
        first, last = pieces_of(phase)[part]
        span = (last - first) * tile_chunks
        for half, (low, high) in enumerate(halves):
            if first <= low and high <= last:
                wait_bytes(orecv.at[phase, pl.ds(low, high - low)], o_recv.at[phase, half])
        for n in range(first, last):
            both = obuf[n, core] + orecv[phase, n].astype(jnp.float32)
            for i in range(tile_chunks):
                at = (n - first) * tile_chunks + i
                xf[pl.ds(at, rows, stride=span), :] = both[:, i * 128 : (i + 1) * 128]

        @pl.loop(0, group)
        def _(q):
            size = cap * span
            block = xf[pl.ds(pl.multiple_of(q * size, 8), size), :].reshape(cap, span, 128)
            snd2[phase, q, :, span_of((first, last))] = block.astype(jnp.bfloat16)

        send_combine(phase, part)

    def over_tiles(phase, body):
        stop = min(n_early + 1, n_out) if phase > 1 else n_out
        pl.loop(0, stop)(body)
        if phase > 1:
            give_back(phase, 0)
        if stop < n_out:
            pl.loop(stop, n_out)(body)

    def await_combine(phase):
        for part, piece in enumerate(pieces_of(phase)):
            wait_bytes(comb[phase].at[:, :, span_of(piece)], comb_recv.at[phase, part])

    def fill_slots(phase, m, source, shift):
        for e in range(n_exp):
            for s in range(cap):
                snd[phase, e, s] = source[m, table[m, e * cap + s] >> shift]

    def picked_of(phase, m, t, k):
        slot = table[m, n_exp * cap + 2 * t + k]
        e, s = slot // cap, lax.rem(slot, cap)
        result = comb[phase][e * n_x, s].astype(jnp.float32)
        for x in range(1, n_x):
            result = result + comb[phase][e * n_x + x, s].astype(jnp.float32)
        return result

    def forward_ready(m):
        @pl.when(section == 1)
        def _():
            hop(acts, lin, 0, m).wait_recv()

        for t in range(toks):
            v = lin[m, t].astype(jnp.float32)
            hidden = (v * inv_rms_of(v) * gain).astype(jnp.bfloat16)
            hid[m, t] = hidden
            gap = total(hidden.astype(jnp.float32) * router_diff(m, t))
            prob[m, t, 0] = jnp.broadcast_to(sigmoid(gap), (8, 128))
            prob[m, t, 1] = jnp.broadcast_to(sigmoid(-gap), (8, 128))
        fill_slots(m, m, hid, 1)

    def forward_expert(m):
        sibling_rows(m)
        if m == 0:
            weights[0].wait()
            weights[1].wait()

        @pl.loop(0, n_ff)
        def _(n):
            cols = pl.ds(pl.multiple_of(n * tile_ff, tile_ff), tile_ff)
            gate = jnp.dot(left(), wg[:, cols], preferred_element_type=jnp.float32)
            gs[m, n] = gate
            up = jnp.dot(left(), wu[:, cols], preferred_element_type=jnp.float32)
            us[m, n] = up
            act[:, cols] = (gate * sigmoid(gate) * up).astype(jnp.bfloat16)

        if m == 0:
            weights[2].wait()

        def out_tile(n):
            cols = pl.ds(pl.multiple_of(n * tile_out, tile_out), tile_out)
            tile = jnp.dot(act[...], wd[:, cols], preferred_element_type=jnp.float32)
            share_tile(m, n, tile)

        over_tiles(m, out_tile)

    def forward_end(m):
        await_combine(m)
        for t in range(toks):
            p0 = prob[m, t, 0, 0:1, 0:1]
            p1 = prob[m, t, 1, 0:1, 0:1]
            one, two = picked_of(m, m, t, 0), picked_of(m, m, t, 1)
            v = lin[m, t].astype(jnp.float32)
            acts[m, t] = (v + (p0 * one + p1 * two)).astype(jnp.bfloat16)
            pdiff[m, t] = one - two

        @pl.when(section == 0)
        def _():
            hop(acts, lin, 0, m).start()

        blocks_to_rows(acts, acts_out, m)

    def backward_send(m):
        phase = 2 + m

        @pl.when(section == 0)
        def _():
            hop(grads, ups, 1, m).wait_recv()

        gaps = []
        for t in range(toks):
            up = ups[m, t].astype(jnp.float32)
            p0 = prob[m, t, 0, 0:1, 0:1]
            p1 = prob[m, t, 1, 0:1, 0:1]
            d_gap = p0 * p1 * total(up * pdiff[m, t])
            prob[m, t, 2] = jnp.broadcast_to(d_gap, (8, 128))
            gaps.append(d_gap)
            scl[m, 2 * t] = (p0 * up).astype(jnp.bfloat16)
            scl[m, 2 * t + 1] = (p1 * up).astype(jnp.bfloat16)
        fill_slots(phase, m, scl, 0)
        send_dispatch(phase)
        for e in range(n_exp):
            term = racc[e] if m else jnp.zeros((chunks, 128), jnp.float32)
            for t in range(toks):
                sign = jnp.where(route(m, t, 0) == e, 1.0, 0.0) - jnp.where(
                    route(m, t, 1) == e, 1.0, 0.0
                )
                term = term + (gaps[t] * sign) * hid[m, t].astype(jnp.float32)
            racc[e] = term
        if m:
            router_one()

    def router_one():
        pltpu.make_async_copy(racc.at[my_e], r1.at[my_e], r_recv.at[0]).start()

        @pl.loop(1, n_exp)
        def _(step):
            e = lax.rem(my_e + step, n_exp)
            pltpu.make_async_remote_copy(
                src_ref=racc.at[e],
                dst_ref=r1.at[my_e],
                send_sem=r_send.at[0],
                recv_sem=r_recv.at[0],
                device_id={"expert": e},
                device_id_type=MESH,
            ).start()

    def router_two():
        wait_bytes(r1, r_recv.at[0])
        rsrc[0] = jnp.sum(r1[...], axis=0)
        pltpu.make_async_copy(rsrc.at[0], r2.at[my_dp], r_recv.at[1]).start()

        @pl.loop(1, 2 * n_x)
        def _(step):
            dp = lax.rem(my_dp + step, 2 * n_x)
            pltpu.make_async_remote_copy(
                src_ref=rsrc.at[0],
                dst_ref=r2.at[my_dp],
                send_sem=r_send.at[1],
                recv_sem=r_recv.at[1],
                device_id={"dp": dp},
                device_id_type=MESH,
            ).start()

    def router_three():
        wait_bytes(r2, r_recv.at[1])
        rsrc[1] = jnp.sum(r2[...], axis=0)
        pltpu.make_async_copy(rsrc.at[1], r3.at[my_e], r_recv.at[2]).start()

        @pl.loop(1, n_exp)
        def _(step):
            e = lax.rem(my_e + step, n_exp)
            pltpu.make_async_remote_copy(
                src_ref=rsrc.at[1],
                dst_ref=r3.at[my_e],
                send_sem=r_send.at[2],
                recv_sem=r_recv.at[2],
                device_id={"expert": e},
                device_id_type=MESH,
            ).start()

    def backward_expert(m):
        phase = 2 + m
        sibling_rows(phase)

        @pl.loop(0, n_ff)
        def _(n):
            part = pl.ds(pl.multiple_of(n * tile_ff, tile_ff), tile_ff)
            d_act = lax.dot_general(
                left(), wd[part, :], NT, preferred_element_type=jnp.float32
            )
            gate, up = gs[m, n], us[m, n]
            sig = sigmoid(gate)
            act[:, part] = (d_act * up * sig * (1.0 + gate * (1.0 - sig))).astype(jnp.bfloat16)
            act2[:, part] = (d_act * gate * sig).astype(jnp.bfloat16)

        if m:
            router_two()

        def back_tile(n):
            part = pl.ds(pl.multiple_of(n * tile_out, tile_out), tile_out)
            tile = lax.dot_general(act[...], wg[part, :], NT, preferred_element_type=jnp.float32)
            tile = tile + lax.dot_general(
                act2[...], wu[part, :], NT, preferred_element_type=jnp.float32
            )
            share_tile(phase, n, tile)

        over_tiles(phase, back_tile)

    def backward_end(m):
        phase = 2 + m
        await_combine(phase)
        for t in range(toks):
            d_gap = prob[m, t, 2, 0:1, 0:1]
            d_hidden = picked_of(phase, m, t, 0) + picked_of(phase, m, t, 1)
            d_hidden = d_hidden + d_gap * router_diff(m, t)
            v = lin[m, t].astype(jnp.float32)
            up = ups[m, t].astype(jnp.float32)
            inv_rms = inv_rms_of(v)
            weighted = gain * d_hidden
            mean = total(v * weighted) * inv_count
            d_in = up + inv_rms * weighted - v * (inv_rms * inv_rms * inv_rms) * mean
            grads[m, t] = d_in.astype(jnp.bfloat16)

        @pl.when(section == 1)
        def _():
            hop(grads, ups, 1, m).start()

        blocks_to_rows(grads, grads_out, m)

    @pl.when(section == 0)
    def _():
        forward_ready(0)

    pl.semaphore_wait(barrier, group + n_x)

    @pl.when(section == 0)
    def _():
        send_dispatch(0)
        forward_ready(1)
        take_rows(0)
        send_dispatch(1)
        forward_expert(0)
        give_back(0, 0)
        take_rows(1)
        forward_expert(1)
        forward_end(0)
        give_back(1, 0)
        forward_end(1)
        backward_send(0)
        backward_send(1)
        take_rows(2)
        backward_expert(0)
        give_back(2, 1)
        take_rows(3)
        backward_expert(1)
        give_back(3, 1)
        router_three()
        backward_end(0)
        backward_end(1)

    @pl.when(section == 1)
    def _():
        forward_ready(0)
        send_dispatch(0)
        forward_ready(1)
        send_dispatch(1)
        take_rows(0)
        forward_expert(0)
        give_back(0, 0)
        take_rows(1)
        forward_expert(1)
        give_back(1, 0)
        forward_end(0)
        backward_send(0)
        forward_end(1)
        backward_send(1)
        take_rows(2)
        backward_expert(0)
        give_back(2, 1)
        take_rows(3)
        backward_expert(1)
        backward_end(0)
        give_back(3, 1)
        router_three()
        backward_end(1)

    wait_bytes(r3, r_recv.at[2])
    for e in range(n_exp):
        flat[pl.ds(e, chunks, stride=n_exp), :] = r3[e]
    for j in range(chunks):
        rgrad[:, j * 128 : (j + 1) * 128] = flat[j * n_exp : (j + 1) * n_exp, :]

    for phase in range(4):
        wait_bytes(disp.at[phase, core, pl.ds(0, group - 1)], disp_send.at[phase])
        for part, piece in enumerate(pieces_of(phase)):
            sent = comb[phase].at[pl.ds(0, group - 1), :, span_of(piece)]
            wait_bytes(sent, comb_send.at[phase, part])
        wait_bytes(disp.at[phase, core], x_send.at[phase])
        wait_bytes(osend.at[phase], o_send.at[phase])
    wait_bytes(r1.at[pl.ds(0, n_exp - 1)], r_send.at[0])
    wait_bytes(r2.at[pl.ds(0, 2 * n_x - 1)], r_send.at[1])
    wait_bytes(r1.at[pl.ds(0, n_exp - 1)], r_send.at[2])
    for m in range(2):

        @pl.when(section == 0)
        def _():
            hop(acts, lin, 0, m).wait_send()

        @pl.when(section == 1)
        def _():
            hop(grads, ups, 1, m).wait_send()


def finish_kernel(acts, grads, rgrad, acts_out, grads_out, rgrad_out):
    acts_out[...] = acts[...]
    grads_out[...] = grads[...]
    rgrad_out[...] = rgrad[...]


def slot_tables(picks, cap, experts):
    micro, toks, top = picks.shape
    flat = picks.reshape(micro, toks * top)
    order = jnp.arange(toks * top, dtype=jnp.int32)
    same = (flat[:, :, None] == flat[:, None, :]) & (order[None, None, :] < order[None, :, None])
    slot_of = flat * cap + jnp.sum(same.astype(jnp.int32), axis=2)
    slots = jnp.arange(experts * cap, dtype=jnp.int32)
    hit = slot_of[:, None, :] == slots[None, :, None]
    gap = toks * top - order
    slot_src = toks * top - jnp.sum(jnp.where(hit, gap[None, None, :], 0), axis=2)
    return jnp.concatenate([slot_src, slot_of, flat], axis=1).astype(jnp.int32)


def per_device(inputs, cotangent, norm_gain, router, w_gate, w_up, w_down, routes):
    micro, toks, width = inputs.shape
    experts = router.shape[2]
    dp = lax.axis_size("dp")
    n_exp, n_x = lax.axis_size("expert"), dp // 2
    cap = 3
    chunks = width // 128
    hidden_units = w_gate.shape[3]
    tile_ff, tile_out = min(TILE_FF, hidden_units), min(TILE_OUT, width)
    n_ff, n_out = hidden_units // tile_ff, width // tile_out
    group = n_exp * n_x
    rows = group * cap
    n_batch = min(4, n_exp)
    table = slot_tables(routes[0], cap, experts)
    bf, f32 = jnp.bfloat16, jnp.float32
    block = (chunks, 128)
    n_early = max(n_out * 2 // 3, 1)
    dma = pltpu.SemaphoreType.DMA
    scratch = [
        pltpu.VMEM((width, hidden_units), bf),
        pltpu.VMEM((width, hidden_units), bf),
        pltpu.VMEM((hidden_units, width), bf),
        pltpu.VMEM((micro, toks) + block, bf),
        pltpu.VMEM((micro, toks) + block, bf),
        pltpu.VMEM(block, f32),
        pltpu.VMEM((experts,) + block, f32),
        pltpu.VMEM((chunks * 8, 128), f32),
        pltpu.VMEM((micro, toks) + block, bf),
        pltpu.VMEM((micro, toks) + block, bf),
        pltpu.VMEM((micro, toks + 1) + block, bf),
        pltpu.VMEM((micro, 2 * toks + 1) + block, bf),
        pltpu.VMEM((micro, toks, 3, 8, 128), f32),
        pltpu.VMEM((micro, toks) + block, f32),
        pltpu.VMEM((4, n_exp, cap) + block, bf),
        pltpu.VMEM((4, 2, group, cap) + block, bf),
        pltpu.VMEM((rows * chunks, 128), f32),
        pltpu.VMEM((2, rows, width), bf),
        pltpu.VMEM((micro, n_ff, 2 * rows, tile_ff), f32),
        pltpu.VMEM((micro, n_ff, 2 * rows, tile_ff), f32),
        pltpu.VMEM((2 * rows, hidden_units), bf),
        pltpu.VMEM((2 * rows, hidden_units), bf),
        pltpu.VMEM((n_out, 2, rows, tile_out), f32),
        pltpu.VMEM((4, n_out, rows, tile_out), bf),
        pltpu.VMEM((4, n_out, rows, tile_out), bf),
        pltpu.VMEM((4, group, cap) + block, bf),
        pltpu.VMEM((group, cap) + block, bf),
        pltpu.VMEM((group, cap) + block, bf),
        pltpu.VMEM((group, cap) + block, bf),
        pltpu.VMEM((group, cap) + block, bf),
        pltpu.VMEM((n_exp,) + block, f32),
        pltpu.VMEM((n_exp,) + block, f32),
        pltpu.VMEM((dp,) + block, f32),
        pltpu.VMEM((n_exp,) + block, f32),
        pltpu.VMEM((2,) + block, f32),
        dma((3,)),
        dma((4,)),
        dma((4, n_batch)),
        dma((4,)),
        dma((4, n_batch)),
        dma((4,)),
        dma((4, 2)),
        dma((4, 2)),
        dma((4, 2)),
        dma((2, micro)),
        dma((2, micro)),
        dma((3,)),
        dma((3,)),
    ]
    dims = (n_exp, n_x, cap, toks, chunks, n_ff, n_out, n_early, n_batch, tile_ff, tile_out)
    vmem = pl.BlockSpec(memory_space=pltpu.VMEM)
    hbm = pl.BlockSpec(memory_space=pl.ANY)
    acts, grads, rgrad = pl.pallas_call(
        lambda *refs: relay_kernel(dims, *refs),
        out_shape=(
            jax.ShapeDtypeStruct((micro, toks, width), bf),
            jax.ShapeDtypeStruct((micro, toks, width), bf),
            jax.ShapeDtypeStruct((experts, width), f32),
        ),
        in_specs=[pl.BlockSpec(memory_space=pltpu.SMEM)] + [vmem] * 4 + [hbm] * 3,
        out_specs=(vmem, vmem, vmem),
        scratch_shapes=scratch,
        compiler_params=pltpu.CompilerParams(
            collective_id=0, has_side_effects=True, vmem_limit_bytes=63 * 1024 * 1024
        ),
        name="relay",
    )(
        table,
        inputs,
        cotangent,
        norm_gain,
        router[0].T,
        w_gate[0, 0],
        w_up[0, 0],
        w_down[0, 0],
    )
    acts, grads, rgrad = pl.pallas_call(
        finish_kernel,
        out_shape=tuple(jax.ShapeDtypeStruct(a.shape, a.dtype) for a in (acts, grads, rgrad)),
        in_specs=[vmem] * 3,
        out_specs=(vmem,) * 3,
        name="finish",
    )(acts, grads, rgrad)
    return (
        acts[None],
        grads[None],
        rgrad.T[None],
    )


def solution(mesh):
    placed = (
        P(None, ("expert", "dp"), None),
        P(None, ("expert", "dp"), None),
        P("section", None),
        P("section", None, None),
        P("section", "expert", None, "dp"),
        P("section", "expert", None, "dp"),
        P("section", "expert", "dp", None),
        P("section", None, ("expert", "dp"), None),
    )
    return jax.shard_map(
        per_device,
        mesh=mesh,
        in_specs=placed,
        out_specs=(
            P("section", None, ("expert", "dp"), None),
            P("section", None, ("expert", "dp"), None),
            P("section", None, None),
        ),
        check_vma=False,
    )
```

```python
import jax
import jax.numpy as jnp
from jax import lax
from jax.experimental import pallas as pl
from jax.experimental.pallas import tpu as pltpu
from jax.sharding import PartitionSpec as P

EPSILON = 1e-05
TILE_FF = 512
TILE_OUT = 512
MESH = pl.DeviceIdType.MESH
NT = (((1,), (1,)), ((), ()))


def sigmoid(x):
    return jax.nn.sigmoid(x)


def relay_kernel(
    dims,
    table,
    x_in,
    cot_in,
    gain_in,
    router_in,
    wg_hbm,
    wu_hbm,
    wd_hbm,
    acts_out,
    grads_out,
    rgrad,
    wg,
    wu,
    wd,
    acts,
    grads,
    gain_f,
    router_f,
    flat,
    lin,
    ups,
    hid,
    scl,
    prob,
    pdiff,
    snd,
    disp,
    xf,
    xb,
    gs,
    us,
    act,
    act2,
    obuf,
    osend,
    orecv,
    snd2,
    comb_0,
    comb_1,
    comb_2,
    comb_3,
    racc,
    r1,
    r2,
    r3,
    rsrc,
    w_sem,
    disp_send,
    disp_recv,
    x_send,
    x_recv,
    o_send,
    o_recv,
    comb_send,
    comb_recv,
    hop_send,
    hop_recv,
    r_send,
    r_recv,
):
    n_exp, n_x, cap, toks, chunks, n_ff, n_out, n_early, n_batch, tile_ff, tile_out = dims
    group = n_exp * n_x
    rows = group * cap
    per_x = cap * chunks
    inv_count = 1.0 / (chunks * 128)
    batch = group // n_batch
    none = 2 * toks

    section = lax.axis_index("section")
    my_e = lax.axis_index("expert")
    my_dp = lax.axis_index("dp")
    my_x = my_dp // 2
    core = lax.rem(my_dp, 2)
    me = my_e * n_x + my_x

    comb = (comb_0, comb_1, comb_2, comb_3)
    tile_chunks = tile_out // 128
    halves = ((0, n_early), (n_early, n_out))

    def pieces_of(phase):
        return ((0, n_out),) if phase < 2 else halves

    def span_of(piece):
        return pl.ds(piece[0] * tile_chunks, (piece[1] - piece[0]) * tile_chunks)

    def wrapped(value, size):
        return jnp.where(value >= size, value - size, value)

    ahead = [wrapped(my_x + dx, n_x) * 2 + core for dx in range(n_x)]
    behind = [wrapped(my_x + n_x - dx, n_x) * 2 + core for dx in range(n_x)]

    def each_step(body, back=False):
        columns = behind if back else ahead
        for dx in range(1, n_x):
            body(0, dx, my_e, {"expert": my_e, "dp": columns[dx]})

        @pl.loop(1, n_exp)
        def _(de):
            e = wrapped(my_e + n_exp - de if back else my_e + de, n_exp)
            for dx in range(n_x):
                body(de, dx, e, {"expert": e, "dp": columns[dx]})

    sibling = {"dp": my_x * 2 + 1 - core}
    partner = {"section": 1 - section}

    weights = [
        pltpu.make_async_copy(src, dst, w_sem.at[i])
        for i, (src, dst) in enumerate(((wg_hbm, wg), (wu_hbm, wu), (wd_hbm, wd)))
    ]
    for copy in weights:
        copy.start()

    barrier = pltpu.get_barrier_semaphore()

    def greet(de, dx, e, where):
        pl.semaphore_signal(barrier, inc=1, device_id=where, device_id_type=MESH)

    each_step(greet)

    @pl.loop(0, n_x)
    def _(x):
        pl.semaphore_signal(
            barrier, inc=1, device_id={"dp": x * 2 + 1 - core}, device_id_type=MESH
        )

    pl.semaphore_signal(barrier, inc=1, device_id=partner, device_id_type=MESH)

    def rows_to_blocks(source, target):
        for m in range(2):
            for j in range(chunks):
                piece = source[m, :, j * 128 : (j + 1) * 128]
                flat[j * toks : (j + 1) * toks, :] = piece.astype(jnp.float32)
            for t in range(toks):
                target[m, t] = flat[pl.ds(t, chunks, stride=toks), :].astype(jnp.bfloat16)

    def blocks_to_rows(source, target, m):
        for t in range(toks):
            flat[pl.ds(t, chunks, stride=toks), :] = source[m, t].astype(jnp.float32)
        for j in range(chunks):
            piece = flat[j * toks : (j + 1) * toks, :]
            target[m, :, j * 128 : (j + 1) * 128] = piece.astype(jnp.bfloat16)

    @pl.when(section == 0)
    def _():
        rows_to_blocks(x_in, lin)

    @pl.when(section == 1)
    def _():
        rows_to_blocks(cot_in, ups)

    for j in range(chunks):
        gain_f[j : j + 1, :] = gain_in[0:1, j * 128 : (j + 1) * 128].astype(jnp.float32)
    for j in range(chunks):
        piece = router_in[:, j * 128 : (j + 1) * 128]
        flat[j * n_exp : (j + 1) * n_exp, :] = piece.astype(jnp.float32)
    for e in range(n_exp):
        router_f[e] = flat[pl.ds(e, chunks, stride=n_exp), :]

    hid[:, toks] = jnp.zeros_like(hid[:, toks])
    scl[:, none] = jnp.zeros_like(scl[:, none])
    gain = gain_f[...]

    def total(v):
        return jnp.sum(v, axis=(0, 1), keepdims=True)

    def inv_rms_of(v):
        return lax.rsqrt(total(v * v) * inv_count + EPSILON)

    def wait_bytes(ref, sem):
        pltpu.make_async_copy(ref, ref, sem).wait()

    def route(m, t, k):
        return table[m, n_exp * cap + none + 2 * t + k]

    def router_diff(m, t):
        return router_f[route(m, t, 0)] - router_f[route(m, t, 1)]

    def send_dispatch(phase):
        pltpu.make_async_copy(
            snd.at[phase, my_e], disp.at[phase, core, 0], disp_recv.at[phase, 0]
        ).start()

        def send(de, dx, e, where):
            pltpu.make_async_remote_copy(
                src_ref=snd.at[phase, e],
                dst_ref=disp.at[phase, core, de * n_x + dx],
                send_sem=disp_send.at[phase],
                recv_sem=disp_recv.at[phase, de // (batch // n_x)],
                device_id=where,
                device_id_type=MESH,
            ).start()

        each_step(send)

    def send_combine(phase, part):
        span = span_of(pieces_of(phase)[part])
        pltpu.make_async_copy(
            snd2.at[phase, 0, :, span], comb[phase].at[me, :, span], comb_recv.at[phase, part]
        ).start()

        def send(de, dx, e, where):
            pltpu.make_async_remote_copy(
                src_ref=snd2.at[phase, de * n_x + dx, :, span],
                dst_ref=comb[phase].at[me, :, span],
                send_sem=comb_send.at[phase, part],
                recv_sem=comb_recv.at[phase, part],
                device_id=where,
                device_id_type=MESH,
            ).start()

        each_step(send, back=True)

    def hop(ref, dst, which, m):
        return pltpu.make_async_remote_copy(
            src_ref=ref.at[m],
            dst_ref=dst.at[m],
            send_sem=hop_send.at[which, m],
            recv_sem=hop_recv.at[which, m],
            device_id=partner,
            device_id_type=MESH,
        )

    def batch_of(phase, half, b):
        return disp.at[phase, half, pl.ds(b * batch, batch)]

    def unpack(phase, half, b):
        @pl.loop(b * batch, (b + 1) * batch)
        def _(q):
            block = disp[phase, half, q].astype(jnp.float32).reshape(per_x, 128)
            xf[pl.ds(pl.multiple_of(q * per_x, 8), per_x), :] = block

    def to_rows(half):
        for j in range(chunks):
            part = xf[pl.ds(j, rows, stride=chunks), :]
            xb[half, :, j * 128 : (j + 1) * 128] = part.astype(jnp.bfloat16)

    def take_rows(phase):
        for b in range(n_batch):
            wait_bytes(batch_of(phase, core, b), disp_recv.at[phase, b])
            pltpu.make_async_remote_copy(
                src_ref=batch_of(phase, core, b),
                dst_ref=batch_of(phase, core, b),
                send_sem=x_send.at[phase],
                recv_sem=x_recv.at[phase, b],
                device_id=sibling,
                device_id_type=MESH,
            ).start()
            unpack(phase, core, b)
        to_rows(core)

    def sibling_rows(phase):
        for b in range(n_batch):
            wait_bytes(batch_of(phase, 1 - core, b), x_recv.at[phase, b])
            unpack(phase, 1 - core, b)
        to_rows(1 - core)

    def left():
        return xb[...].reshape(2 * rows, chunks * 128)

    def share_tile(phase, n, tile):
        obuf[n] = tile.reshape(2, rows, tile_out)
        osend[phase, n] = obuf[n, 1 - core].astype(jnp.bfloat16)
        pltpu.make_async_remote_copy(
            src_ref=osend.at[phase, n],
            dst_ref=orecv.at[phase, n],
            send_sem=o_send.at[phase],
            recv_sem=o_recv.at[phase, n // n_early],
            device_id=sibling,
            device_id_type=MESH,
        ).start()

    def give_back(phase, part):
        first, last = pieces_of(phase)[part]
        span = (last - first) * tile_chunks
        for half, (low, high) in enumerate(halves):
            if first <= low and high <= last:
                wait_bytes(orecv.at[phase, pl.ds(low, high - low)], o_recv.at[phase, half])
        for n in range(first, last):
            both = obuf[n, core] + orecv[phase, n].astype(jnp.float32)
            for i in range(tile_chunks):
                at = (n - first) * tile_chunks + i
                xf[pl.ds(at, rows, stride=span), :] = both[:, i * 128 : (i + 1) * 128]

        @pl.loop(0, group)
        def _(q):
            size = cap * span
            block = xf[pl.ds(pl.multiple_of(q * size, 8), size), :].reshape(cap, span, 128)
            snd2[phase, q, :, span_of((first, last))] = block.astype(jnp.bfloat16)

        send_combine(phase, part)

    def over_tiles(phase, body, between=None):
        stop = min(n_early + 1, n_out) if phase > 1 else n_out
        pl.loop(0, stop)(body)
        if between is not None:
            between()
        if phase > 1:
            give_back(phase, 0)
        if stop < n_out:
            pl.loop(stop, n_out)(body)

    def await_combine(phase):
        for part, piece in enumerate(pieces_of(phase)):
            wait_bytes(comb[phase].at[:, :, span_of(piece)], comb_recv.at[phase, part])

    def fill_slots(phase, m, source, shift):
        for e in range(n_exp):
            for s in range(cap):
                snd[phase, e, s] = source[m, table[m, e * cap + s] >> shift]

    def picked_of(phase, m, t, k):
        slot = table[m, n_exp * cap + 2 * t + k]
        e, s = slot // cap, lax.rem(slot, cap)
        result = comb[phase][e * n_x, s].astype(jnp.float32)
        for x in range(1, n_x):
            result = result + comb[phase][e * n_x + x, s].astype(jnp.float32)
        return result

    def forward_ready(m):
        @pl.when(section == 1)
        def _():
            hop(acts, lin, 0, m).wait_recv()

        for t in range(toks):
            v = lin[m, t].astype(jnp.float32)
            hidden = (v * inv_rms_of(v) * gain).astype(jnp.bfloat16)
            hid[m, t] = hidden
            gap = total(hidden.astype(jnp.float32) * router_diff(m, t))
            prob[m, t, 0] = jnp.broadcast_to(sigmoid(gap), (8, 128))
            prob[m, t, 1] = jnp.broadcast_to(sigmoid(-gap), (8, 128))
        fill_slots(m, m, hid, 1)

    def forward_expert(m):
        sibling_rows(m)
        if m == 0:
            weights[0].wait()
            weights[1].wait()

        @pl.loop(0, n_ff)
        def _(n):
            cols = pl.ds(pl.multiple_of(n * tile_ff, tile_ff), tile_ff)
            gate = jnp.dot(left(), wg[:, cols], preferred_element_type=jnp.float32)
            gs[m, n] = gate
            up = jnp.dot(left(), wu[:, cols], preferred_element_type=jnp.float32)
            us[m, n] = up
            act[:, cols] = (gate * sigmoid(gate) * up).astype(jnp.bfloat16)

        if m == 0:
            weights[2].wait()

        def out_tile(n):
            cols = pl.ds(pl.multiple_of(n * tile_out, tile_out), tile_out)
            tile = jnp.dot(act[...], wd[:, cols], preferred_element_type=jnp.float32)
            share_tile(m, n, tile)

        over_tiles(m, out_tile)

    def forward_end(m):
        await_combine(m)
        for t in range(toks):
            p0 = prob[m, t, 0, 0:1, 0:1]
            p1 = prob[m, t, 1, 0:1, 0:1]
            one, two = picked_of(m, m, t, 0), picked_of(m, m, t, 1)
            v = lin[m, t].astype(jnp.float32)
            acts[m, t] = (v + (p0 * one + p1 * two)).astype(jnp.bfloat16)
            pdiff[m, t] = one - two

        @pl.when(section == 0)
        def _():
            hop(acts, lin, 0, m).start()

        blocks_to_rows(acts, acts_out, m)

    def backward_send(m):
        phase = 2 + m

        @pl.when(section == 0)
        def _():
            hop(grads, ups, 1, m).wait_recv()

        gaps = []
        for t in range(toks):
            up = ups[m, t].astype(jnp.float32)
            p0 = prob[m, t, 0, 0:1, 0:1]
            p1 = prob[m, t, 1, 0:1, 0:1]
            d_gap = p0 * p1 * total(up * pdiff[m, t])
            prob[m, t, 2] = jnp.broadcast_to(d_gap, (8, 128))
            gaps.append(d_gap)
            scl[m, 2 * t] = (p0 * up).astype(jnp.bfloat16)
            scl[m, 2 * t + 1] = (p1 * up).astype(jnp.bfloat16)
        fill_slots(phase, m, scl, 0)
        send_dispatch(phase)
        for e in range(n_exp):
            term = racc[e] if m else jnp.zeros((chunks, 128), jnp.float32)
            for t in range(toks):
                sign = jnp.where(route(m, t, 0) == e, 1.0, 0.0) - jnp.where(
                    route(m, t, 1) == e, 1.0, 0.0
                )
                term = term + (gaps[t] * sign) * hid[m, t].astype(jnp.float32)
            racc[e] = term
        if m:
            router_one()

    def router_one():
        pltpu.make_async_copy(racc.at[my_e], r1.at[my_e], r_recv.at[0]).start()

        @pl.loop(1, n_exp)
        def _(step):
            e = lax.rem(my_e + step, n_exp)
            pltpu.make_async_remote_copy(
                src_ref=racc.at[e],
                dst_ref=r1.at[my_e],
                send_sem=r_send.at[0],
                recv_sem=r_recv.at[0],
                device_id={"expert": e},
                device_id_type=MESH,
            ).start()

    def router_two():
        wait_bytes(r1, r_recv.at[0])
        rsrc[0] = jnp.sum(r1[...], axis=0)
        pltpu.make_async_copy(rsrc.at[0], r2.at[my_dp], r_recv.at[1]).start()

        @pl.loop(1, 2 * n_x)
        def _(step):
            dp = lax.rem(my_dp + step, 2 * n_x)
            pltpu.make_async_remote_copy(
                src_ref=rsrc.at[0],
                dst_ref=r2.at[my_dp],
                send_sem=r_send.at[1],
                recv_sem=r_recv.at[1],
                device_id={"dp": dp},
                device_id_type=MESH,
            ).start()

    def router_three():
        wait_bytes(r2, r_recv.at[1])
        rsrc[1] = jnp.sum(r2[...], axis=0)
        pltpu.make_async_copy(rsrc.at[1], r3.at[my_e], r_recv.at[2]).start()

        @pl.loop(1, n_exp)
        def _(step):
            e = lax.rem(my_e + step, n_exp)
            pltpu.make_async_remote_copy(
                src_ref=rsrc.at[1],
                dst_ref=r3.at[my_e],
                send_sem=r_send.at[2],
                recv_sem=r_recv.at[2],
                device_id={"expert": e},
                device_id_type=MESH,
            ).start()

    def backward_expert(m, between=None):
        phase = 2 + m
        sibling_rows(phase)

        @pl.loop(0, n_ff)
        def _(n):
            part = pl.ds(pl.multiple_of(n * tile_ff, tile_ff), tile_ff)
            d_act = lax.dot_general(
                left(), wd[part, :], NT, preferred_element_type=jnp.float32
            )
            gate, up = gs[m, n], us[m, n]
            sig = sigmoid(gate)
            act[:, part] = (d_act * up * sig * (1.0 + gate * (1.0 - sig))).astype(jnp.bfloat16)
            act2[:, part] = (d_act * gate * sig).astype(jnp.bfloat16)

        if m:
            router_two()

        def back_tile(n):
            part = pl.ds(pl.multiple_of(n * tile_out, tile_out), tile_out)
            tile = lax.dot_general(act[...], wg[part, :], NT, preferred_element_type=jnp.float32)
            tile = tile + lax.dot_general(
                act2[...], wu[part, :], NT, preferred_element_type=jnp.float32
            )
            share_tile(phase, n, tile)

        over_tiles(phase, back_tile, between)

    def backward_end(m):
        phase = 2 + m
        await_combine(phase)
        for t in range(toks):
            d_gap = prob[m, t, 2, 0:1, 0:1]
            d_hidden = picked_of(phase, m, t, 0) + picked_of(phase, m, t, 1)
            d_hidden = d_hidden + d_gap * router_diff(m, t)
            v = lin[m, t].astype(jnp.float32)
            up = ups[m, t].astype(jnp.float32)
            inv_rms = inv_rms_of(v)
            weighted = gain * d_hidden
            mean = total(v * weighted) * inv_count
            d_in = up + inv_rms * weighted - v * (inv_rms * inv_rms * inv_rms) * mean
            grads[m, t] = d_in.astype(jnp.bfloat16)

        @pl.when(section == 1)
        def _():
            hop(grads, ups, 1, m).start()

        blocks_to_rows(grads, grads_out, m)

    @pl.when(section == 0)
    def _():
        forward_ready(0)

    pl.semaphore_wait(barrier, group + n_x)

    @pl.when(section == 0)
    def _():
        send_dispatch(0)
        forward_ready(1)
        take_rows(0)
        send_dispatch(1)
        forward_expert(0)
        give_back(0, 0)
        take_rows(1)
        forward_expert(1)
        forward_end(0)
        give_back(1, 0)
        forward_end(1)
        backward_send(0)
        backward_send(1)
        take_rows(2)
        backward_expert(0)
        give_back(2, 1)
        take_rows(3)
        backward_expert(1)
        give_back(3, 1)
        router_three()
        backward_end(0)
        backward_end(1)

    @pl.when(section == 1)
    def _():
        forward_ready(0)
        send_dispatch(0)
        forward_ready(1)
        send_dispatch(1)
        take_rows(0)
        forward_expert(0)
        give_back(0, 0)
        take_rows(1)
        forward_expert(1)
        give_back(1, 0)
        forward_end(0)
        backward_send(0)
        forward_end(1)
        backward_send(1)
        take_rows(2)
        backward_expert(0)
        give_back(2, 1)
        take_rows(3)
        backward_expert(1, lambda: backward_end(0))
        give_back(3, 1)
        router_three()
        backward_end(1)

    wait_bytes(r3, r_recv.at[2])
    for e in range(n_exp):
        flat[pl.ds(e, chunks, stride=n_exp), :] = r3[e]
    for j in range(chunks):
        rgrad[:, j * 128 : (j + 1) * 128] = flat[j * n_exp : (j + 1) * n_exp, :]

    for phase in range(4):
        wait_bytes(disp.at[phase, core, pl.ds(0, group - 1)], disp_send.at[phase])
        for part, piece in enumerate(pieces_of(phase)):
            sent = comb[phase].at[pl.ds(0, group - 1), :, span_of(piece)]
            wait_bytes(sent, comb_send.at[phase, part])
        wait_bytes(disp.at[phase, core], x_send.at[phase])
        wait_bytes(osend.at[phase], o_send.at[phase])
    wait_bytes(r1.at[pl.ds(0, n_exp - 1)], r_send.at[0])
    wait_bytes(r2.at[pl.ds(0, 2 * n_x - 1)], r_send.at[1])
    wait_bytes(r1.at[pl.ds(0, n_exp - 1)], r_send.at[2])
    for m in range(2):

        @pl.when(section == 0)
        def _():
            hop(acts, lin, 0, m).wait_send()

        @pl.when(section == 1)
        def _():
            hop(grads, ups, 1, m).wait_send()


def finish_kernel(acts, grads, rgrad, acts_out, grads_out, rgrad_out):
    acts_out[...] = acts[...]
    grads_out[...] = grads[...]
    rgrad_out[...] = rgrad[...]


def slot_tables(picks, cap, experts):
    micro, toks, top = picks.shape
    flat = picks.reshape(micro, toks * top)
    order = jnp.arange(toks * top, dtype=jnp.int32)
    same = (flat[:, :, None] == flat[:, None, :]) & (order[None, None, :] < order[None, :, None])
    slot_of = flat * cap + jnp.sum(same.astype(jnp.int32), axis=2)
    slots = jnp.arange(experts * cap, dtype=jnp.int32)
    hit = slot_of[:, None, :] == slots[None, :, None]
    gap = toks * top - order
    slot_src = toks * top - jnp.sum(jnp.where(hit, gap[None, None, :], 0), axis=2)
    return jnp.concatenate([slot_src, slot_of, flat], axis=1).astype(jnp.int32)


def per_device(inputs, cotangent, norm_gain, router, w_gate, w_up, w_down, routes):
    micro, toks, width = inputs.shape
    experts = router.shape[2]
    dp = lax.axis_size("dp")
    n_exp, n_x = lax.axis_size("expert"), dp // 2
    cap = 3
    chunks = width // 128
    hidden_units = w_gate.shape[3]
    tile_ff, tile_out = min(TILE_FF, hidden_units), min(TILE_OUT, width)
    n_ff, n_out = hidden_units // tile_ff, width // tile_out
    group = n_exp * n_x
    rows = group * cap
    n_batch = min(4, n_exp)
    table = slot_tables(routes[0], cap, experts)
    bf, f32 = jnp.bfloat16, jnp.float32
    block = (chunks, 128)
    n_early = max(n_out * 2 // 3, 1)
    dma = pltpu.SemaphoreType.DMA
    scratch = [
        pltpu.VMEM((width, hidden_units), bf),
        pltpu.VMEM((width, hidden_units), bf),
        pltpu.VMEM((hidden_units, width), bf),
        pltpu.VMEM((micro, toks) + block, bf),
        pltpu.VMEM((micro, toks) + block, bf),
        pltpu.VMEM(block, f32),
        pltpu.VMEM((experts,) + block, f32),
        pltpu.VMEM((chunks * 8, 128), f32),
        pltpu.VMEM((micro, toks) + block, bf),
        pltpu.VMEM((micro, toks) + block, bf),
        pltpu.VMEM((micro, toks + 1) + block, bf),
        pltpu.VMEM((micro, 2 * toks + 1) + block, bf),
        pltpu.VMEM((micro, toks, 3, 8, 128), f32),
        pltpu.VMEM((micro, toks) + block, f32),
        pltpu.VMEM((4, n_exp, cap) + block, bf),
        pltpu.VMEM((4, 2, group, cap) + block, bf),
        pltpu.VMEM((rows * chunks, 128), f32),
        pltpu.VMEM((2, rows, width), bf),
        pltpu.VMEM((micro, n_ff, 2 * rows, tile_ff), f32),
        pltpu.VMEM((micro, n_ff, 2 * rows, tile_ff), f32),
        pltpu.VMEM((2 * rows, hidden_units), bf),
        pltpu.VMEM((2 * rows, hidden_units), bf),
        pltpu.VMEM((n_out, 2, rows, tile_out), f32),
        pltpu.VMEM((4, n_out, rows, tile_out), bf),
        pltpu.VMEM((4, n_out, rows, tile_out), bf),
        pltpu.VMEM((4, group, cap) + block, bf),
        pltpu.VMEM((group, cap) + block, bf),
        pltpu.VMEM((group, cap) + block, bf),
        pltpu.VMEM((group, cap) + block, bf),
        pltpu.VMEM((group, cap) + block, bf),
        pltpu.VMEM((n_exp,) + block, f32),
        pltpu.VMEM((n_exp,) + block, f32),
        pltpu.VMEM((dp,) + block, f32),
        pltpu.VMEM((n_exp,) + block, f32),
        pltpu.VMEM((2,) + block, f32),
        dma((3,)),
        dma((4,)),
        dma((4, n_batch)),
        dma((4,)),
        dma((4, n_batch)),
        dma((4,)),
        dma((4, 2)),
        dma((4, 2)),
        dma((4, 2)),
        dma((2, micro)),
        dma((2, micro)),
        dma((3,)),
        dma((3,)),
    ]
    dims = (n_exp, n_x, cap, toks, chunks, n_ff, n_out, n_early, n_batch, tile_ff, tile_out)
    vmem = pl.BlockSpec(memory_space=pltpu.VMEM)
    hbm = pl.BlockSpec(memory_space=pl.ANY)
    acts, grads, rgrad = pl.pallas_call(
        lambda *refs: relay_kernel(dims, *refs),
        out_shape=(
            jax.ShapeDtypeStruct((micro, toks, width), bf),
            jax.ShapeDtypeStruct((micro, toks, width), bf),
            jax.ShapeDtypeStruct((experts, width), f32),
        ),
        in_specs=[pl.BlockSpec(memory_space=pltpu.SMEM)] + [vmem] * 4 + [hbm] * 3,
        out_specs=(vmem, vmem, vmem),
        scratch_shapes=scratch,
        compiler_params=pltpu.CompilerParams(
            collective_id=0, has_side_effects=True, vmem_limit_bytes=63 * 1024 * 1024
        ),
        name="relay",
    )(
        table,
        inputs,
        cotangent,
        norm_gain,
        router[0].T,
        w_gate[0, 0],
        w_up[0, 0],
        w_down[0, 0],
    )
    acts, grads, rgrad = pl.pallas_call(
        finish_kernel,
        out_shape=tuple(jax.ShapeDtypeStruct(a.shape, a.dtype) for a in (acts, grads, rgrad)),
        in_specs=[vmem] * 3,
        out_specs=(vmem,) * 3,
        name="finish",
    )(acts, grads, rgrad)
    return (
        acts[None],
        grads[None],
        rgrad.T[None],
    )


def solution(mesh):
    placed = (
        P(None, ("expert", "dp"), None),
        P(None, ("expert", "dp"), None),
        P("section", None),
        P("section", None, None),
        P("section", "expert", None, "dp"),
        P("section", "expert", None, "dp"),
        P("section", "expert", "dp", None),
        P("section", None, ("expert", "dp"), None),
    )
    return jax.shard_map(
        per_device,
        mesh=mesh,
        in_specs=placed,
        out_specs=(
            P("section", None, ("expert", "dp"), None),
            P("section", None, ("expert", "dp"), None),
            P("section", None, None),
        ),
        check_vma=False,
    )
```
